256 devices in a mesh: section: 8 (over z), expert: 8 (over y_hi, x), dp: 4 (over y_lo, core).
Axes of the slice: x: 4, y: 4 (y_hi: 2, y_lo: 2; y = y_hi * 2 + y_lo), z: 8, core: 2. Of those that a mesh axis runs over, the one named last changes fastest.
Arguments:
- tokens: bfloat16 [8, 256, 4096], P('section', None, ('expert', 'dp'))
- targets: bfloat16 [8, 256, 4096], P('section', None, ('expert', 'dp')), may hold values from -6 to 6
- group_ids: int32 [8, 256], P('section'), may hold values from 0 to 7, as said below
- expert_ids: int32 [1, 8, 8, 256, 2], P(None, 'section'), may hold values from 0 to 7, all different within a row; in each aligned block of 256 rows (0 to 255, 256 to 511, ..., all dimensions but the last counted through in order) at most 72 rows name the same one
- norm_gain: float32 [8, 4096], P('section', ('expert', 'dp')), may hold values from 0.5 to 1.5
- router: bfloat16 [8, 4096, 8], P('section', ('expert', 'dp')), may hold values from -0.09375 to 0.09375
- w_gate: bfloat16 [8, 8, 4096, 1536], P('section', 'expert', None, 'dp'), may hold values from -0.09375 to 0.09375
- w_up: bfloat16 [8, 8, 4096, 1536], P('section', 'expert', None, 'dp'), may hold values from -0.09375 to 0.09375
- w_down: bfloat16 [8, 8, 1536, 4096], P('section', 'expert', 'dp'), may hold values from -0.15625 to 0.15625
Outputs:
- grad_out: bfloat16 [8, 256, 4096], P('section', None, ('expert', 'dp'))
- group_loss: float32 [8], replicated
The draws below stay inside these ranges and needn't reach their ends.
Inputs may be any that keep to these rules, and one draw needn't show every extreme that they name: `expert_ids`: in each aligned block of 256 rows (one micro-batch at one layer pass) no expert is named by more than 72 rows; a row names 2 different experts. `group_ids`: exactly one group has no rows; which one varies.
All inputs are finite; a program needn't handle non-finite values.
Results may differ from the reference program's by a relative error of at most 0.019.
Values may be sent and summed in bfloat16 or wider, within the bound.
A program may use at most 64 MiB of HBM per device.

```python
import math
import jax
import jax.numpy as jnp
import numpy as np
from jax import lax

D = 4096
FFE = 1536
ROWS = 256
CIRCUITS = 1
GROUPS = 8
TOPK = 2
SECTIONS = 8
EXPERTS = 8
CAP = 72
N_DP = 4


def draw_tokens(key, part):
    first_key = jax.random.fold_in(jax.random.fold_in(key, 17), 0)
    total_rows = SECTIONS * ROWS
    row_place = jnp.arange(total_rows, dtype=jnp.float32) / max(total_rows - 1, 1)
    column_place = jnp.arange(D, dtype=jnp.float32) / max(D - 1, 1)
    scales = (1.0 + row_place)[:, None] * (1.0 + column_place)[None, :]
    values = jax.random.normal(first_key, (total_rows, D), jnp.float32) * scales
    return values.reshape(SECTIONS, ROWS, D).astype(jnp.bfloat16)


def draw_group_ids(key, part):
    empty_key, first_key, second_key, low_key, high_key = jax.random.split(jax.random.fold_in(key, 29), 5)
    total_rows = SECTIONS * ROWS
    half_rows = total_rows // 2
    empty_group = jax.random.randint(empty_key, (), 1, GROUPS - 1, dtype=jnp.int32)
    first_label = jax.random.randint(first_key, (total_rows,), 0, GROUPS - 1, dtype=jnp.int32)
    second_label = jax.random.randint(second_key, (total_rows,), 0, GROUPS - 1, dtype=jnp.int32)
    labels = jnp.minimum(first_label, second_label)
    low_place = jax.random.randint(low_key, (), 0, half_rows, dtype=jnp.int32)
    high_place = jax.random.randint(high_key, (), half_rows, total_rows, dtype=jnp.int32)
    labels = labels.at[low_place].set(0)
    labels = labels.at[high_place].set(GROUPS - 2)
    groups = labels + (labels >= empty_group).astype(jnp.int32)
    return groups.reshape(SECTIONS, ROWS).astype(jnp.int32)


def level_of(key, shape, cuts, least, largest):
    loudness = 1.0
    for axis_at, shards_of in cuts:
        steps = jax.random.uniform(jax.random.fold_in(jax.random.fold_in(key, 6), axis_at), (shards_of,), jnp.float32, least / len(cuts), largest / len(cuts))
        loudness = loudness * jnp.repeat(jnp.exp(steps), shape[axis_at] // shards_of).reshape((-1,) + (1,) * (len(shape) - 1 - axis_at))
    return loudness


def deal_out(rng, own, number, rows, count, top, most, slope):
    order = jax.random.permutation(rng, count)
    heavy_load, usual = shares(count, rows * top, most, slope, True), shares(count, rows * top, most, slope, False)
    places = jnp.arange(count)

    def named(tallies, turn):
        used = int((tallies > 0).sum())
        fixed = max(1, used // 4)
        passed = fixed + (places - fixed + turn * (used - fixed)) % max(1, count - fixed)
        return jnp.zeros((count,), jnp.int32).at[order[jnp.where(places < fixed, places, passed)]].set(jnp.asarray(tallies, jnp.int32))

    tallies = jnp.where(number % 4 == 0, named(heavy_load, number // 4), named(usual, number - number // 4 - 1))
    mixed = jax.random.permutation(jax.random.fold_in(own, 3), count)
    donor, taker = mixed[0:count // 2 * 2:2], mixed[1:count // 2 * 2:2]
    margin = jnp.minimum(tallies[donor] - 1, most - tallies[taker]) // 2
    margin = jnp.where((donor == order[0]) | (taker == order[0]) | (tallies[taker] == 0), 0, jnp.maximum(margin, 0))
    passed = jax.random.randint(jax.random.fold_in(own, 4), (count // 2,), 0, 1 << 20) % (margin + 1)
    tallies = tallies.at[donor].add(-passed).at[taker].add(passed)
    members = jnp.searchsorted(jnp.cumsum(tallies), jnp.arange(rows * top), side="right").astype(jnp.int32)
    table = members.reshape(top, rows).T
    table = table[jax.random.permutation(jax.random.fold_in(own, 1), rows)]
    turn = jax.random.randint(jax.random.fold_in(own, 2), (rows, 1), 0, top)
    return jnp.take_along_axis(table, (jnp.arange(top)[None, :] + turn) % top, axis=1)


def shares(number_of, total, most, slope, full):
    portions = [(1 << 20) // math.isqrt(rank ** slope) + 1 for rank in range(1, number_of + 1)]
    largest = most if full else min(most, max(-(-total // number_of), total * portions[0] // sum(portions)))
    least = 1 if total - largest >= number_of - 1 else 0
    holding, surplus = [largest] + [least] * (number_of - 1), total - largest - least * (number_of - 1)
    while surplus > 0:
        movable = [i for i in range(1, number_of) if holding[i] < largest] or [i for i in range(1, number_of) if holding[i] < most]
        pool, budget = sum([portions[i] for i in movable]), surplus
        for i in movable:
            addition = min(most - holding[i], max(1, budget * portions[i] // pool), surplus)
            holding[i] = holding[i] + addition
            surplus = surplus - addition
    return np.array(holding)


def centred(key, dims, scale, limit, cuts=(), kind=jnp.bfloat16):
    level = level_of(key, dims, cuts, -0.22, 0.18) if cuts else 1.0
    entries = jax.random.normal(key, dims, jnp.float32) * scale * level
    return jnp.minimum(jnp.maximum(entries, -limit), limit).astype(kind)


def setup_inputs(seed: int = 0) -> dict:
    streams_of = jax.random.split(jax.random.key(seed), 10)
    tokens = draw_tokens(jax.random.fold_in(streams_of[9], 71), 0)
    targets = centred(streams_of[1], (SECTIONS, ROWS, D), 1.0, 6.0, ((0, 8), (2, 32)))
    group_ids = draw_group_ids(jax.random.fold_in(streams_of[9], 71), 0)
    expert_ids_keys = jax.random.split(jax.random.fold_in(streams_of[3], 1), CIRCUITS * SECTIONS * SECTIONS * ROWS // ROWS)
    expert_ids_turns = jax.random.permutation(jax.random.fold_in(streams_of[3], 3), CIRCUITS * SECTIONS * SECTIONS * ROWS // ROWS)
    expert_ids = jax.vmap(lambda own, number: deal_out(jax.random.fold_in(streams_of[3], 2), own, number, ROWS, EXPERTS, TOPK, CAP, 2))(expert_ids_keys, expert_ids_turns).reshape((CIRCUITS, SECTIONS, SECTIONS, ROWS, TOPK))
    norm_gain = jnp.clip(1.0 + 0.1 * jax.random.normal(streams_of[4], (SECTIONS, D), jnp.float32), 0.5, 1.5)
    router = centred(streams_of[5], (SECTIONS, D, EXPERTS), D ** -0.5, 0.09375, ((0, 8), (1, 32)))
    w_gate = centred(streams_of[6], (SECTIONS, EXPERTS, D, FFE), D ** -0.5, 0.09375, ((0, 8), (1, 8), (3, 4)))
    w_up = centred(streams_of[7], (SECTIONS, EXPERTS, D, FFE), D ** -0.5, 0.09375, ((0, 8), (1, 8), (3, 4)))
    w_down = centred(streams_of[8], (SECTIONS, EXPERTS, FFE, D), FFE ** -0.5, 0.15625, ((0, 8), (1, 8), (2, 4)))
    return {"tokens": tokens, "targets": targets, "group_ids": group_ids, "expert_ids": expert_ids, "norm_gain": norm_gain, "router": router, "w_gate": w_gate, "w_up": w_up, "w_down": w_down}


dro_rate = 0.3

def expert_block(inputs):
    hidden_rows, gate_matrix, up_matrix, down_matrix = inputs
    gate_part = jnp.dot(hidden_rows, gate_matrix, preferred_element_type=jnp.float32)
    up_part = jnp.dot(hidden_rows, up_matrix, preferred_element_type=jnp.float32)
    activated = (jax.nn.silu(gate_part) * up_part).astype(jnp.bfloat16)
    lane_width = FFE // N_DP
    summed = jnp.zeros((hidden_rows.shape[0], D), jnp.float32)
    for lane_index in range(N_DP):
        lane_piece = jnp.dot(activated[:, lane_index * lane_width:(lane_index + 1) * lane_width], down_matrix[lane_index * lane_width:(lane_index + 1) * lane_width], preferred_element_type=jnp.float32).astype(jnp.bfloat16)
        summed = summed + lane_piece.astype(jnp.float32)
    return summed

def layer_pass(hidden_state, choices, gain_row, router_matrix, gate_stack, up_stack, down_stack):
    wide_state = hidden_state.astype(jnp.float32)
    row_scale = lax.rsqrt(lax.optimization_barrier(jnp.mean(wide_state * wide_state, axis=1, keepdims=True)) + 1e-06)
    normed = (wide_state * row_scale * gain_row[None, :]).astype(jnp.bfloat16)
    logits = jnp.dot(normed, router_matrix, preferred_element_type=jnp.float32)
    chosen = jnp.take_along_axis(logits, choices, axis=1)
    weights = jnp.exp(chosen)
    gate_weights = weights / lax.optimization_barrier(jnp.sum(weights, axis=1, keepdims=True))
    flat_choice = choices.reshape(-1).astype(jnp.int32)
    member = (flat_choice[:, None] == jnp.arange(EXPERTS, dtype=jnp.int32)[None, :]).astype(jnp.int32)
    rank_before = jnp.cumsum(member, axis=0) - member
    position = lax.optimization_barrier(jnp.sum(rank_before * member, axis=1)).astype(jnp.int32)
    slot_index = (flat_choice * CAP + position).astype(jnp.int32)
    source = (jnp.arange(flat_choice.shape[0], dtype=jnp.int32) // TOPK).astype(jnp.int32)
    slot_table = jnp.full((EXPERTS * CAP,), hidden_state.shape[0], jnp.int32).at[slot_index].set(source)
    padded = jnp.concatenate([normed, jnp.zeros((1, D), jnp.bfloat16)], axis=0)
    grouped = padded[slot_table].reshape(EXPERTS, CAP, D)
    results = lax.map(expert_block, (grouped, gate_stack, up_stack, down_stack))
    picked = results.reshape(-1, D)[slot_index]
    mixture = lax.optimization_barrier(jnp.sum(picked.reshape(-1, TOPK, D) * gate_weights[:, :, None], axis=1))
    return (wide_state + mixture).astype(jnp.bfloat16)

def reference(tokens, targets, group_ids, expert_ids, norm_gain, router, w_gate, w_up, w_down):
    finals = []
    for micro_index in range(SECTIONS):
        hidden_state = tokens[micro_index]
        for pass_index in range(CIRCUITS * SECTIONS):
            layer_index = (micro_index + pass_index) % SECTIONS
            circuit = pass_index // SECTIONS
            choices = expert_ids[circuit, layer_index, micro_index]
            hidden_state = layer_pass(hidden_state, choices, norm_gain[layer_index], router[layer_index], w_gate[layer_index], w_up[layer_index], w_down[layer_index])
        finals.append(hidden_state)
    final_state = jnp.stack(finals).reshape(-1, D)
    difference = final_state.astype(jnp.float32) - targets.reshape(-1, D).astype(jnp.float32)
    loss_row = lax.optimization_barrier(jnp.mean(difference * difference, axis=1))
    group_flat = group_ids.reshape(-1)
    member = (group_flat[:, None] == jnp.arange(GROUPS, dtype=jnp.int32)[None, :]).astype(jnp.float32)
    totals = jnp.dot(loss_row, member, precision=lax.Precision.HIGHEST)
    counts = lax.optimization_barrier(jnp.sum(member, axis=0))
    group_loss = totals / jnp.maximum(counts, 1.0)
    raised = jnp.exp(dro_rate * group_loss)
    group_weight = raised / jnp.sum(raised)
    row_weight_table = group_weight * (SECTIONS * ROWS) / jnp.maximum(counts, 1.0)
    row_weight = jnp.dot(member, row_weight_table, precision=lax.Precision.HIGHEST)
    grad_out = (row_weight[:, None] * difference).astype(jnp.bfloat16).reshape(SECTIONS, ROWS, D)
    return (grad_out, group_loss)
```

```python
import functools

import jax
import jax.numpy as jnp
from jax import lax
from jax.experimental import pallas as pl
from jax.experimental.pallas import tpu as pltpu
from jax.sharding import PartitionSpec as P

MESH = pl.DeviceIdType.MESH
GROUPS = 8
TOPK = 2
DRO_RATE = 0.3
LANES = 128
F32 = jnp.float32
BF16 = jnp.bfloat16
LAST_DIMS = (((1,), (1,)), ((), ()))


def dot(a, b):
    return jnp.dot(a, b, preferred_element_type=F32)


def dot_t(a, b):
    return lax.dot_general(a, b, LAST_DIMS, preferred_element_type=F32)


def ones_where(mask):
    return jnp.where(mask, 1.0, 0.0).astype(BF16)


def kernel(
    sections, experts, slots, per_group, width,
    tok_ref, tgt_ref, gid_ref, ids_ref, gain_ref, rt_ref, wg_ref, wu_ref, wd_ref,
    grad_ref, loss_ref,
    w_gu, w_dn, x_all, x_new, out_buf, x_in, acc, sq_acc, logit_acc, act, dn_acc, part_out, part_in,
    pick, scat, member, columns, upper, eye, rt_mine, rt_in, rt_bf, red_mine, red_in, red_sib, red_z,
    w_sem, wd_sem, wd_send, wd_recv, d_send, d_recv, f_send, f_recv, a_send, a_recv,
    c_send, c_recv, z_send, z_recv, r_send, r_recv, rf_send, rf_recv, s_send, s_recv,
    sb_send, sb_recv, sz_send, sz_recv,
):
    chips = experts * 2
    rows = tok_ref.shape[0]
    hidden = wg_ref.shape[-1]
    section = lax.axis_index("section")
    expert = lax.axis_index("expert")
    lane = lax.axis_index("dp")
    core = lax.rem(lane, 2)
    half = lane // 2
    mine = expert * 2 + half
    other = 1 - core
    sibling = (section, expert, half * 2 + other)

    def peer(step):
        place = lax.rem(mine + step, chips)
        return place, (section, place // 2, lax.rem(place, 2) * 2 + core)

    def source(step):
        return lax.rem(mine + chips - step, chips)

    def along_z(step):
        return (lax.rem(section + step, sections), expert, lane)

    def remote(src, dst, send, recv, device):
        return pltpu.make_async_remote_copy(
            src_ref=src, dst_ref=dst, send_sem=send, recv_sem=recv, device_id=device, device_id_type=MESH
        )

    loads = []
    for side in range(2):
        loads.append(pltpu.make_async_copy(wg_ref.at[:, side], w_gu.at[side, :, :, 0:hidden], w_sem.at[2 * side]))
        loads.append(
            pltpu.make_async_copy(wu_ref.at[:, side], w_gu.at[side, :, :, hidden : 2 * hidden], w_sem.at[2 * side + 1])
        )
    for j in range(chips):
        own_columns = pl.ds(pl.multiple_of(j * 2 * LANES + core * LANES, LANES), LANES)
        loads.append(pltpu.make_async_copy(wd_ref.at[:, own_columns], w_dn.at[core, j], wd_sem.at[j]))
    for load in loads:
        load.start()

    barrier = pltpu.get_barrier_semaphore()
    for step in range(1, chips):
        pl.semaphore_signal(barrier, inc=1, device_id=peer(step)[1], device_id_type=MESH)
    pl.semaphore_signal(barrier, inc=1, device_id=sibling, device_id_type=MESH)
    for step in range(1, sections):
        pl.semaphore_signal(barrier, inc=1, device_id=along_z(step), device_id_type=MESH)

    gain = gain_ref[...]
    rt_mine[0:8, :] = rt_ref[...]
    rt_mine[8:16, :] = jnp.broadcast_to(1.0 / (gain * gain), (8, LANES))
    rt_in[core, 0] = rt_mine[...]
    first = lax.broadcasted_iota(jnp.int32, (rows, rows), 0)
    second = lax.broadcasted_iota(jnp.int32, (rows, rows), 1)
    upper[...] = ones_where(first < second)
    eye[...] = ones_where(first == second)
    x_all[0] = tok_ref[...]

    expert_rows = lax.broadcasted_iota(jnp.int32, (16, rows), 0)

    def prepare_pick(moment):
        micro = lax.rem(section + 2 * sections - moment, sections)
        first_id = ids_ref[micro, 0:1, :]
        second_id = ids_ref[micro, 1:2, :]
        hit_first = first_id == expert_rows
        hit_second = second_id == expert_rows
        either = hit_first | hit_second
        named = ones_where(either)
        rank = dot(named, upper[...])
        member[...] = named
        rank_first = jnp.sum(jnp.where(hit_first, rank, 0.0), axis=0, keepdims=True)
        rank_second = jnp.sum(jnp.where(hit_second, rank, 0.0), axis=0, keepdims=True)
        table = jnp.where(expert_rows == 0, first_id.astype(F32), second_id.astype(F32))
        table = jnp.where(expert_rows == 2, rank_first, table)
        table = jnp.where(expert_rows == 3, rank_second, table)
        columns[...] = table.astype(BF16)
        key = jnp.where(either, rank, -1.0)
        slot_rows = lax.broadcasted_iota(jnp.int32, (slots, rows), 0).astype(F32)
        for e in range(experts):
            pick[e * slots : (e + 1) * slots, :] = ones_where(key[e : e + 1, :] == slot_rows)

    def prepare_scatter():
        spread = dot_t(eye[...], columns[...])
        slot_first = spread[:, 0:1] * slots + spread[:, 2:3]
        slot_second = spread[:, 1:2] * slots + spread[:, 3:4]
        lanes = lax.broadcasted_iota(jnp.int32, (rows, LANES), 1).astype(F32)
        for n in range(experts * slots // LANES):
            here = lanes + float(n * LANES)
            scat[:, n * LANES : (n + 1) * LANES] = ones_where((slot_first == here) | (slot_second == here))

    prepare_pick(0)

    pl.semaphore_wait(barrier, chips + sections - 1)

    for step in range(1, chips):
        remote(rt_mine, rt_in.at[core, step], r_send.at[step], r_recv.at[step], peer(step)[1]).start()
    for j in range(chips):
        sib_columns = pl.ds(pl.multiple_of(j * 2 * LANES + other * LANES, LANES), LANES)
        remote(wd_ref.at[:, sib_columns], w_dn.at[core, j], wd_send.at[j], wd_recv.at[j], sibling).start()

    def dispatch(moment):
        scaled = (x_all[moment].astype(F32) * gain).astype(BF16)
        out_buf[...] = dot(pick[...], scaled).astype(BF16)
        for step in range(1, chips):
            place, device = peer(step)
            block = pl.ds(pl.multiple_of((place // 2) * slots, 16), slots)
            remote(out_buf.at[block, :], x_in.at[core, step], d_send.at[step], d_recv.at[step], device).start()
        own_block = pl.ds(pl.multiple_of(expert * slots, 16), slots)
        x_in[core, 0] = out_buf[own_block, :]

    def router_blocks():
        for step in range(1, chips):
            copy = remote(rt_mine, rt_in.at[core, step], r_send.at[step], r_recv.at[step], peer(step)[1])
            copy.wait_recv()
            copy.wait_send()
        forward = remote(rt_in.at[core], rt_in.at[core], rf_send.at[0], rf_recv.at[0], sibling)
        forward.start()
        forward.wait_send()
        remote(rt_in.at[other], rt_in.at[other], rf_send.at[0], rf_recv.at[0], sibling).wait_recv()
        for side in range(2):
            for step in range(chips):
                rt_bf[side, :, step * LANES : (step + 1) * LANES] = rt_in[side, step].astype(BF16)

    def weights_here():
        for load in loads:
            load.wait()
        for j in range(chips):
            copy = remote(
                wd_ref.at[:, pl.ds(0, LANES)], w_dn.at[other, j], wd_send.at[j], wd_recv.at[j], sibling
            )
            copy.wait_send()
            copy.wait_recv()

    group_count = chips // per_group

    def group_work(side, g, fresh):
        steps = range(g * per_group, (g + 1) * per_group)
        blocks = [x_in[side, step] for step in steps]
        block = jnp.concatenate(blocks, axis=1)
        weight = jnp.concatenate([w_gu[side, source(step)] for step in steps], axis=0)
        product = dot(block, weight)
        router = rt_bf[side, :, g * per_group * LANES : (g + 1) * per_group * LANES]
        logits = dot_t(block, router)
        squares = None
        for step, piece in zip(steps, blocks):
            wide = piece.astype(F32)
            term = wide * wide * rt_in[side, step, 8:9, :]
            squares = term if squares is None else squares + term
        if fresh:
            acc[...] = product
            logit_acc[...] = logits
            sq_acc[...] = squares
        else:
            acc[...] += product
            logit_acc[...] += logits
            sq_acc[...] += squares

    def own_group(g, fresh=False):
        for step in range(max(1, g * per_group), (g + 1) * per_group):
            remote(
                out_buf.at[pl.ds(0, slots), :], x_in.at[core, step], d_send.at[step], d_recv.at[step], sibling
            ).wait_recv()
        block = pl.ds(g * per_group, per_group)
        remote(x_in.at[core, block], x_in.at[core, block], f_send.at[g], f_recv.at[g], sibling).start()
        group_work(core, g, fresh)

    def sibling_group(g):
        block = pl.ds(g * per_group, per_group)
        remote(x_in.at[other, block], x_in.at[other, block], f_send.at[g], f_recv.at[g], sibling).wait_recv()
        group_work(other, g, False)

    def tick(moment, carry):
        dispatch(moment)
        prepare_scatter()

        @pl.when(moment == 0)
        def _():
            router_blocks()
            weights_here()

        own_group(0, True)
        for g in range(1, group_count):
            own_group(g)
            sibling_group(g - 1)
        sibling_group(group_count - 1)

        row_scale = lax.rsqrt(jnp.sum(sq_acc[...], axis=1, keepdims=True) / width + 1e-6)
        gate_part = acc[:, 0:hidden] * row_scale
        up_part = acc[:, hidden : 2 * hidden] * row_scale
        act[core] = (gate_part / (1.0 + jnp.exp(-gate_part)) * up_part).astype(BF16)
        swap = remote(act.at[core], act.at[core], a_send.at[0], a_recv.at[0], sibling)
        swap.start()

        own_pick = pick[pl.ds(pl.multiple_of(expert * slots, 16), slots), :]
        chosen = dot_t(own_pick, member[...]) > 0.5
        logits = logit_acc[...] * row_scale
        lanes = lax.broadcasted_iota(jnp.int32, (slots, 16), 1)
        top = jnp.max(jnp.where(chosen, logits, -1e30), axis=1, keepdims=True)
        raised = jnp.where(chosen, jnp.exp(jnp.where(chosen, logits - top, 0.0)), 0.0)
        gate = jnp.sum(jnp.where(lanes == expert, raised, 0.0), axis=1, keepdims=True) / jnp.maximum(
            jnp.sum(raised, axis=1, keepdims=True), 1e-30
        )

        orders = [(step, (step + 1) % chips) for step in range(1, chips, 2)]

        def down_weight(side, pair):
            return jnp.concatenate([w_dn[side, lax.rem(mine + step, chips)] for step in pair], axis=1)

        own_act = act[core]
        for i, pair in enumerate(orders):
            dn_acc[i] = dot(own_act, down_weight(core, pair))
        for g in range(group_count):
            block = pl.ds(g * per_group, per_group)
            remote(x_in.at[core, block], x_in.at[core, block], f_send.at[g], f_recv.at[g], sibling).wait_send()
        for step in range(1, chips):
            remote(
                out_buf.at[pl.ds(0, slots), :], x_in.at[core, step], d_send.at[step], d_recv.at[step], sibling
            ).wait_send()
        remote(act.at[other], act.at[other], a_send.at[0], a_recv.at[0], sibling).wait_recv()
        swap.wait_send()
        sib_act = act[other]
        landing = pl.ds(pl.multiple_of((half * experts + expert) * slots, 16), slots)
        for i, pair in enumerate(orders):
            piece = ((dn_acc[i] + dot(sib_act, down_weight(other, pair))) * gate).astype(BF16)
            for at, step in enumerate(pair):
                value = piece[:, at * LANES : (at + 1) * LANES]
                if step == 0:
                    part_in[landing, :] = value
                else:
                    part_out[step] = value
                    remote(
                        part_out.at[step], part_in.at[landing, :], c_send.at[step], c_recv.at[step], peer(step)[1]
                    ).start()

        prepare_pick(moment + 1)

        for step in range(1, chips):
            copy = remote(
                part_out.at[step], part_in.at[pl.ds(0, slots), :], c_send.at[step], c_recv.at[step], sibling
            )
            copy.wait_recv()
            copy.wait_send()
        table = scat[...]
        count = experts * slots
        moe = dot(table, part_in[0:count, :]) + dot(table, part_in[count : 2 * count, :])
        x_new[...] = (x_all[moment].astype(F32) + moe).astype(BF16)
        onward = remote(x_new, x_all.at[moment + 1], z_send.at[0], z_recv.at[moment], along_z(1))
        onward.start()
        onward.wait_send()
        onward.wait_recv()
        return carry

    lax.fori_loop(0, sections, tick, 0)

    difference = x_all[sections].astype(F32) - tgt_ref[...].astype(F32)
    row_loss = jnp.sum(difference * difference, axis=1, keepdims=True) / width
    group_row = gid_ref[...]
    group_column = dot_t(eye[...], jnp.broadcast_to(group_row.astype(F32), (16, rows)).astype(BF16))[:, 0:1]
    lanes = lax.broadcasted_iota(jnp.int32, (rows, LANES), 1).astype(F32)
    belongs = jnp.where(group_column == lanes, 1.0, 0.0)
    totals = jnp.sum(belongs * row_loss, axis=0, keepdims=True)
    counts = jnp.sum(belongs, axis=0, keepdims=True)
    red_rows = lax.broadcasted_iota(jnp.int32, (8, LANES), 0)
    local = jnp.where(red_rows == 0, totals, counts)
    red_mine[0] = local
    red_in[mine] = local
    for step in range(1, chips):
        remote(red_mine.at[0], red_in.at[mine], s_send.at[step], s_recv.at[step], peer(step)[1]).start()
    for step in range(1, chips):
        copy = remote(red_mine.at[0], red_in.at[source(step)], s_send.at[step], s_recv.at[step], peer(step)[1])
        copy.wait_recv()
        copy.wait_send()
    plane = red_in[0]
    for j in range(1, chips):
        plane = plane + red_in[j]
    red_mine[1] = plane
    across = remote(red_mine.at[1], red_sib, sb_send.at[0], sb_recv.at[0], sibling)
    across.start()
    across.wait_send()
    across.wait_recv()
    both = plane + red_sib[...]
    red_mine[2] = both
    red_z[section] = both
    for step in range(1, sections):
        remote(red_mine.at[2], red_z.at[section], sz_send.at[step], sz_recv.at[step], along_z(step)).start()
    for step in range(1, sections):
        there = lax.rem(section + sections - step, sections)
        copy = remote(red_mine.at[2], red_z.at[there], sz_send.at[step], sz_recv.at[step], along_z(step))
        copy.wait_recv()
        copy.wait_send()
    whole = red_z[0]
    for j in range(1, sections):
        whole = whole + red_z[j]
    total = whole[0:1, :]
    count = whole[1:2, :] / (chips * 2)
    safe = jnp.maximum(count, 1.0)
    group_loss = total / safe
    lane_row = lax.broadcasted_iota(jnp.int32, (1, LANES), 1)
    raised = jnp.where(lane_row < GROUPS, jnp.exp(DRO_RATE * group_loss), 0.0)
    weight = raised / jnp.sum(raised, axis=1, keepdims=True) * (sections * rows) / safe
    row_weight = jnp.sum(belongs * weight, axis=1, keepdims=True)
    grad_ref[...] = (row_weight * difference).astype(BF16)
    loss_ref[...] = jnp.broadcast_to(group_loss, (8, LANES))


def per_device(slots, per_group, tokens, targets, group_ids, expert_ids, norm_gain, router, w_gate, w_up, w_down):
    sections = lax.axis_size("section")
    experts = lax.axis_size("expert")
    chips = experts * 2
    rows = tokens.shape[1]
    width = w_gate.shape[2]
    hidden = w_gate.shape[3]
    ids = jnp.transpose(expert_ids[0, 0], (0, 2, 1))
    router_rows = jnp.zeros((8, LANES), F32).at[:experts].set(jnp.transpose(router[0].astype(F32)))
    vmem = pl.BlockSpec(memory_space=pltpu.VMEM)
    anywhere = pl.BlockSpec(memory_space=pl.ANY)
    dma = pltpu.SemaphoreType.DMA
    scratch = [
        pltpu.VMEM((2, chips, LANES, 2 * hidden), BF16),
        pltpu.VMEM((2, chips, hidden, LANES), BF16),
        pltpu.VMEM((sections + 1, rows, LANES), BF16),
        pltpu.VMEM((rows, LANES), BF16),
        pltpu.VMEM((experts * slots, LANES), BF16),
        pltpu.VMEM((2, chips, slots, LANES), BF16),
        pltpu.VMEM((slots, 2 * hidden), F32),
        pltpu.VMEM((slots, LANES), F32),
        pltpu.VMEM((slots, 16), F32),
        pltpu.VMEM((2, slots, hidden), BF16),
        pltpu.VMEM((chips // 2, slots, 2 * LANES), F32),
        pltpu.VMEM((chips, slots, LANES), BF16),
        pltpu.VMEM((chips * slots, LANES), BF16),
        pltpu.VMEM((experts * slots, rows), BF16),
        pltpu.VMEM((rows, experts * slots), BF16),
        pltpu.VMEM((16, rows), BF16),
        pltpu.VMEM((16, rows), BF16),
        pltpu.VMEM((rows, rows), BF16),
        pltpu.VMEM((rows, rows), BF16),
        pltpu.VMEM((16, LANES), F32),
        pltpu.VMEM((2, chips, 16, LANES), F32),
        pltpu.VMEM((2, 16, chips * LANES), BF16),
        pltpu.VMEM((3, 8, LANES), F32),
        pltpu.VMEM((chips, 8, LANES), F32),
        pltpu.VMEM((8, LANES), F32),
        pltpu.VMEM((sections, 8, LANES), F32),
        dma((4,)),
        dma((chips,)),
        dma((chips,)),
        dma((chips,)),
        dma((chips,)),
        dma((chips,)),
        dma((chips // per_group,)),
        dma((chips // per_group,)),
        dma((1,)),
        dma((1,)),
        dma((chips,)),
        dma((chips,)),
        dma((1,)),
        dma((sections,)),
        dma((chips,)),
        dma((chips,)),
        dma((1,)),
        dma((1,)),
        dma((chips,)),
        dma((chips,)),
        dma((1,)),
        dma((1,)),
        dma((sections,)),
        dma((sections,)),
    ]
    grad, loss = pl.pallas_call(
        functools.partial(kernel, sections, experts, slots, per_group, float(width)),
        out_shape=(
            jax.ShapeDtypeStruct((rows, LANES), BF16),
            jax.ShapeDtypeStruct((8, LANES), F32),
        ),
        in_specs=[vmem] * 6 + [anywhere] * 3,
        out_specs=(vmem, vmem),
        scratch_shapes=scratch,
        compiler_params=pltpu.CompilerParams(
            collective_id=0, has_side_effects=True, vmem_limit_bytes=60 * 1024 * 1024
        ),
        name="moe_ring",
    )(
        tokens[0],
        targets[0],
        group_ids,
        ids,
        norm_gain,
        router_rows,
        w_gate.reshape(chips, 2, LANES, hidden),
        w_up.reshape(chips, 2, LANES, hidden),
        w_down.reshape(hidden, width),
    )
    return grad[None], loss[0, :GROUPS]


def build(mesh, slots, per_group):
    placed = (
        P("section", None, ("expert", "dp")),
        P("section", None, ("expert", "dp")),
        P("section", None),
        P(None, "section", None, None, None),
        P("section", ("expert", "dp")),
        P("section", ("expert", "dp"), None),
        P("section", "expert", None, "dp"),
        P("section", "expert", None, "dp"),
        P("section", "expert", "dp", None),
    )
    return jax.shard_map(
        functools.partial(per_device, slots, per_group),
        mesh=mesh,
        in_specs=placed,
        out_specs=(P("section", None, ("expert", "dp")), P()),
        check_vma=False,
    )


def solution(mesh):
    return build(mesh, 80, 4)
```

```python
import functools

import jax
import jax.numpy as jnp
from jax import lax
from jax.experimental import pallas as pl
from jax.experimental.pallas import tpu as pltpu
from jax.sharding import PartitionSpec as P

MESH = pl.DeviceIdType.MESH
GROUPS = 8
TOPK = 2
DRO_RATE = 0.3
LANES = 128
F32 = jnp.float32
BF16 = jnp.bfloat16
LAST_DIMS = (((1,), (1,)), ((), ()))


def dot(a, b):
    return jnp.dot(a, b, preferred_element_type=F32)


def dot_t(a, b):
    return lax.dot_general(a, b, LAST_DIMS, preferred_element_type=F32)


def ones_where(mask):
    return jnp.where(mask, 1.0, 0.0).astype(BF16)


def kernel(
    sections, experts, slots, sent, per_group, width,
    tok_ref, tgt_ref, gid_ref, ids_ref, gain_ref, rt_ref, wg_ref, wu_ref, wd_ref,
    grad_ref, loss_ref,
    w_gu, w_dn, x_all, x_res, out_buf, x_in, acc, sq_acc, logit_acc, act, dn_acc, part_out, part_in,
    tgt, gid, ids, ids_before, gain_row, rt_raw,
    pick, scat, member, upper, eye, rt_mine, rt_in, rt_bf, red_mine, red_in, red_z,
    in_sem, w_sem, wd_sem, wd_send, wd_recv, d_send, d_recv, f_send, f_recv, a_send, a_recv,
    c_send, c_recv, z_send, z_recv, r_send, r_recv, rf_send, rf_recv, i_send, i_recv, s_send, s_recv,
    sz_send, sz_recv,
):
    chips = experts * 2
    across = 4
    down = chips // across
    rows = tok_ref.shape[0]
    hidden = wg_ref.shape[-1]
    section = lax.axis_index("section")
    expert = lax.axis_index("expert")
    lane = lax.axis_index("dp")
    core = lax.rem(lane, 2)
    half = lane // 2
    x_place = lax.rem(expert, across)
    y_place = expert // across * 2 + half
    mine = expert * 2 + half
    other = 1 - core
    sibling = (section, expert, half * 2 + other)

    def hops(offset):
        return min(offset[0], across - offset[0]) + min(offset[1], down - offset[1])

    offsets = [(dx, dy) for dx in range(across) for dy in range(down)]
    order = [(0, 0)] + sorted(offsets[1:], key=lambda offset: -hops(offset))
    sends = order[1:] + order[:1]

    def chip(offset, sign=1):
        x = lax.rem(x_place + across + sign * offset[0], across)
        y = lax.rem(y_place + down + sign * offset[1], down)
        return y // 2 * across + x, lax.rem(y, 2)

    def place_of(offset, sign=1):
        e, h = chip(offset, sign)
        return e * 2 + h

    def device(offset, on=0, swap=0):
        e, h = chip(offset)
        return (lax.rem(section + on, sections), e, h * 2 + (other if swap else core))

    def remote(src, dst, send, recv, target):
        return pltpu.make_async_remote_copy(
            src_ref=src, dst_ref=dst, send_sem=send, recv_sem=recv, device_id=target, device_id_type=MESH
        )

    inputs = [
        pltpu.make_async_copy(src, dst, in_sem.at[n])
        for n, (src, dst) in enumerate(
            [(ids_ref, ids), (tok_ref, x_all.at[0]), (gain_ref, gain_row), (rt_ref, rt_raw), (tgt_ref, tgt), (gid_ref, gid)]
        )
    ]
    loads = []
    for side in range(2):
        loads.append(pltpu.make_async_copy(wg_ref.at[:, side], w_gu.at[side, :, :, 0:hidden], w_sem.at[2 * side]))
        loads.append(
            pltpu.make_async_copy(wu_ref.at[:, side], w_gu.at[side, :, :, hidden : 2 * hidden], w_sem.at[2 * side + 1])
        )
    for j in range(chips):
        own_columns = pl.ds(pl.multiple_of(j * 2 * LANES + core * LANES, LANES), LANES)
        loads.append(pltpu.make_async_copy(wd_ref.at[:, own_columns], w_dn.at[core, j], wd_sem.at[j]))
    for load in inputs + loads:
        load.start()

    part_in[...] = jnp.zeros(part_in.shape, BF16)

    barrier = pltpu.get_barrier_semaphore()
    partners = {(dx, dy, 0, 0) for dx, dy in offsets[1:]} | {(0, 0, 0, 1)}
    partners |= {(dx, dy, dz % sections, 0) for dx, dy in offsets for dz in (1, -1)}
    partners |= {(0, 0, dz, swap) for dz in range(1, sections) for swap in range(2)}
    for dx, dy, dz, swap in sorted(partners):
        pl.semaphore_signal(barrier, inc=1, device_id=device((dx, dy), dz, swap), device_id_type=MESH)

    first = lax.broadcasted_iota(jnp.int32, (rows, rows), 0)
    second = lax.broadcasted_iota(jnp.int32, (rows, rows), 1)
    upper[...] = ones_where(first < second)
    eye[...] = ones_where(first == second)
    for load in inputs:
        load.wait()
    gain = gain_row[...]
    rt_mine[0:8, :] = rt_raw[...].astype(F32)
    rt_mine[8:16, :] = jnp.broadcast_to(1.0 / (gain * gain), (8, LANES))
    rt_in[core, 0] = rt_mine[...]

    expert_rows = lax.broadcasted_iota(jnp.int32, (16, rows), 0)

    def micro_of(moment):
        return lax.rem(section + 2 * sections - moment, sections)

    def ranks(table, micro):
        first_id = table[micro, 0:1, :]
        second_id = table[micro, 1:2, :]
        hit_first = first_id == expert_rows
        hit_second = second_id == expert_rows
        either = hit_first | hit_second
        named = ones_where(either)
        return first_id, second_id, hit_first, hit_second, either, named, dot(named, upper[...])

    def prepare_pick(moment):
        _, _, _, _, either, named, rank = ranks(ids, micro_of(moment))
        member[...] = named
        key = jnp.where(either, rank, -1.0)
        slot_rows = lax.broadcasted_iota(jnp.int32, (slots, rows), 0).astype(F32)
        for e in range(experts):
            pick[e * slots : (e + 1) * slots, :] = ones_where(key[e : e + 1, :] == slot_rows)

    def prepare_scatter(moment):
        first_id, second_id, hit_first, hit_second, _, _, rank = ranks(ids_before, micro_of(moment))
        rank_first = jnp.sum(jnp.where(hit_first, rank, 0.0), axis=0, keepdims=True)
        rank_second = jnp.sum(jnp.where(hit_second, rank, 0.0), axis=0, keepdims=True)
        table = jnp.where(expert_rows == 0, first_id.astype(F32), second_id.astype(F32))
        table = jnp.where(expert_rows == 2, rank_first, table)
        table = jnp.where(expert_rows == 3, rank_second, table)
        spread = dot_t(eye[...], table.astype(BF16))
        slot_first = spread[:, 0:1] * slots + spread[:, 2:3]
        slot_second = spread[:, 1:2] * slots + spread[:, 3:4]
        lanes = lax.broadcasted_iota(jnp.int32, (rows, LANES), 1).astype(F32)
        for n in range(experts * slots // LANES):
            here = lanes + float(n * LANES)
            scat[:, n * LANES : (n + 1) * LANES] = ones_where((slot_first == here) | (slot_second == here))

    prepare_pick(0)

    pl.semaphore_wait(barrier, len(partners))

    def router_copy(k):
        return remote(rt_mine, rt_in.at[core, k], r_send.at[k], r_recv.at[k], device(order[k]))

    ids_copy = remote(ids, ids_before, i_send.at[0], i_recv.at[0], device((0, 0), 1))

    def down_copy(j):
        sib_columns = pl.ds(pl.multiple_of(j * 2 * LANES + other * LANES, LANES), LANES)
        return remote(wd_ref.at[:, sib_columns], w_dn.at[core, j], wd_send.at[j], wd_recv.at[j], sibling)

    for k in range(1, chips):
        router_copy(k).start()
    ids_copy.start()

    def dispatch_copy(k, side):
        e, _ = chip(order[k])
        block = pl.ds(pl.multiple_of(e * slots, 16), sent)
        return remote(
            out_buf.at[block, :], x_in.at[side, core, k, pl.ds(0, sent)], d_send.at[k], d_recv.at[side, k],
            device(order[k]),
        )

    def dispatch(moment, side):
        scaled = (x_all[moment].astype(F32) * gain).astype(BF16)
        out_buf[...] = dot(pick[...], scaled).astype(BF16)
        for k in range(1, chips):
            dispatch_copy(k, side).start()
        own_block = pl.ds(pl.multiple_of(expert * slots, 16), slots)
        x_in[side, core, 0] = out_buf[own_block, :]

    def first_tick():
        for j in range(chips):
            down_copy(j).start()
        for k in range(1, chips):
            copy = router_copy(k)
            copy.wait_recv()
            copy.wait_send()
        forward = remote(rt_in.at[core], rt_in.at[core], rf_send.at[0], rf_recv.at[0], sibling)
        forward.start()
        ids_copy.wait_recv()
        ids_copy.wait_send()
        forward.wait_send()
        remote(rt_in.at[other], rt_in.at[other], rf_send.at[0], rf_recv.at[0], sibling).wait_recv()
        for side in range(2):
            for k in range(chips):
                rt_bf[side, :, k * LANES : (k + 1) * LANES] = rt_in[side, k].astype(BF16)
        for load in loads:
            load.wait()

    def down_here():
        for j in range(chips):
            copy = remote(wd_ref.at[:, pl.ds(0, LANES)], w_dn.at[other, j], wd_send.at[j], wd_recv.at[j], sibling)
            copy.wait_send()
            copy.wait_recv()

    group_count = chips // per_group

    def group_work(side, source, g, fresh):
        ks = range(g * per_group, (g + 1) * per_group)
        blocks = [x_in[side, source, k] for k in ks]
        block = jnp.concatenate(blocks, axis=1)
        weight = jnp.concatenate([w_gu[source, place_of(order[k], -1)] for k in ks], axis=0)
        product = dot(block, weight)
        router = rt_bf[source, :, g * per_group * LANES : (g + 1) * per_group * LANES]
        logits = dot_t(block, router)
        squares = None
        for k, piece in zip(ks, blocks):
            wide = piece.astype(F32)
            term = wide * wide * rt_in[source, k, 8:9, :]
            squares = term if squares is None else squares + term
        if fresh:
            acc[...] = product
            logit_acc[...] = logits
            sq_acc[...] = squares
        else:
            acc[...] += product
            logit_acc[...] += logits
            sq_acc[...] += squares

    def forward_copy(source, g, side):
        block = x_in.at[side, source, pl.ds(g * per_group, per_group)]
        return remote(block, block, f_send.at[g], f_recv.at[side, g], sibling)

    def own_group(g, side, fresh=False):
        for k in range(max(1, g * per_group), (g + 1) * per_group):
            dispatch_copy(k, side).wait_recv()
        forward_copy(core, g, side).start()
        group_work(side, core, g, fresh)

    def sibling_group(g, side):
        forward_copy(other, g, side).wait_recv()
        group_work(side, other, g, False)

    pairs = [(n, n + 1) for n in range(0, chips, 2)]

    def tick(moment, carry):
        side = lax.rem(moment, 2)
        dispatch(moment, side)
        ahead = remote(
            x_all.at[moment], x_res.at[moment], z_send.at[0], z_recv.at[moment], device((0, 0), 1)
        )
        ahead.start()

        @pl.when(moment == 0)
        def _():
            first_tick()

        prepare_scatter(moment + 1)

        own_group(0, side, True)
        for g in range(1, group_count):
            own_group(g, side)
            sibling_group(g - 1, side)
        sibling_group(group_count - 1, side)

        row_scale = lax.rsqrt(jnp.sum(sq_acc[...], axis=1, keepdims=True) / width + 1e-6)
        gate_part = acc[:, 0:hidden] * row_scale
        up_part = acc[:, hidden : 2 * hidden] * row_scale
        act[core] = (gate_part / (1.0 + jnp.exp(-gate_part)) * up_part).astype(BF16)
        swap = remote(act.at[core], act.at[core], a_send.at[0], a_recv.at[0], sibling)
        swap.start()

        own_pick = pick[pl.ds(pl.multiple_of(expert * slots, 16), slots), :]
        chosen = dot_t(own_pick, member[...]) > 0.5
        logits = logit_acc[...] * row_scale
        lanes = lax.broadcasted_iota(jnp.int32, (slots, 16), 1)
        top = jnp.max(jnp.where(chosen, logits, -1e30), axis=1, keepdims=True)
        raised = jnp.where(chosen, jnp.exp(jnp.where(chosen, logits - top, 0.0)), 0.0)
        gate = jnp.sum(jnp.where(lanes == expert, raised, 0.0), axis=1, keepdims=True) / jnp.maximum(
            jnp.sum(raised, axis=1, keepdims=True), 1e-30
        )

        def down_weight(source, pair):
            return jnp.concatenate([w_dn[source, place_of(sends[n])] for n in pair], axis=1)

        own_act = act[core]
        for i, pair in enumerate(pairs):
            dn_acc[i] = dot(own_act, down_weight(core, pair))
        for g in range(group_count):
            forward_copy(core, g, side).wait_send()
        for k in range(1, chips):
            dispatch_copy(k, side).wait_send()

        @pl.when(moment == 0)
        def _():
            down_here()

        remote(act.at[other], act.at[other], a_send.at[0], a_recv.at[0], sibling).wait_recv()
        swap.wait_send()
        sib_act = act[other]
        landing = half * experts + expert

        def part_copy(n):
            return remote(
                part_out.at[n, pl.ds(0, sent)], part_in.at[moment, landing, pl.ds(0, sent)], c_send.at[n],
                c_recv.at[moment], device(sends[n], 1),
            )

        for i, pair in enumerate(pairs):
            piece = ((dn_acc[i] + dot(sib_act, down_weight(other, pair))) * gate).astype(BF16)
            for at, n in enumerate(pair):
                part_out[n] = piece[:, at * LANES : (at + 1) * LANES]
                part_copy(n).start()

        prepare_pick(moment + 1)

        for n in range(chips):
            part_copy(n).wait_send()
        ahead.wait_send()
        ahead.wait_recv()
        everything = part_in.at[moment, :, pl.ds(0, sent)]
        remote(everything, everything, c_send.at[0], c_recv.at[moment], device((0, 0), 1)).wait_recv()
        table = scat[...]
        count = experts * slots
        parts = part_in[moment].reshape(chips * slots, LANES)
        moe = dot(table, parts[0:count]) + dot(table, parts[count : 2 * count])
        x_all[moment + 1] = (x_res[moment].astype(F32) + moe).astype(BF16)
        return carry

    lax.fori_loop(0, sections, tick, 0)

    difference = x_all[sections].astype(F32) - tgt[...].astype(F32)
    row_loss = jnp.sum(difference * difference, axis=1, keepdims=True) / width
    group_column = dot_t(eye[...], jnp.broadcast_to(gid[...].astype(F32), (16, rows)).astype(BF16))[:, 0:1]
    lanes = lax.broadcasted_iota(jnp.int32, (rows, LANES), 1).astype(F32)
    belongs = jnp.where(group_column == lanes, 1.0, 0.0)
    totals = jnp.sum(belongs * row_loss, axis=0, keepdims=True)
    counts = jnp.sum(belongs, axis=0, keepdims=True)
    red_rows = lax.broadcasted_iota(jnp.int32, (8, LANES), 0)
    local = jnp.where(red_rows == 0, totals, counts)
    red_mine[0] = local
    red_in[mine] = local

    def plane_copy(k, place):
        return remote(red_mine.at[0], red_in.at[place], s_send.at[k], s_recv.at[k], device(order[k]))

    for k in range(1, chips):
        plane_copy(k, mine).start()
    for k in range(1, chips):
        copy = plane_copy(k, place_of(order[k], -1))
        copy.wait_recv()
        copy.wait_send()
    plane = red_in[0]
    for j in range(1, chips):
        plane = plane + red_in[j]
    red_mine[1] = plane
    red_z[core, section] = plane
    steps = [(dz, swap) for dz in range(sections) for swap in range(2) if dz or swap]

    def depth_copy(n, lane_core, place):
        dz, swap = steps[n]
        return remote(
            red_mine.at[1], red_z.at[lane_core, place], sz_send.at[n], sz_recv.at[n], device((0, 0), dz, swap)
        )

    for n in range(len(steps)):
        depth_copy(n, core, section).start()
    for n, (dz, swap) in enumerate(steps):
        copy = depth_copy(n, other if swap else core, lax.rem(section + sections - dz, sections))
        copy.wait_recv()
        copy.wait_send()
    whole = red_z[0, 0]
    for n in range(1, 2 * sections):
        whole = whole + red_z[n // sections, n % sections]
    total = whole[0:1, :]
    count = whole[1:2, :] / (chips * 2)
    safe = jnp.maximum(count, 1.0)
    group_loss = total / safe
    lane_row = lax.broadcasted_iota(jnp.int32, (1, LANES), 1)
    raised = jnp.where(lane_row < GROUPS, jnp.exp(DRO_RATE * group_loss), 0.0)
    weight = raised / jnp.sum(raised, axis=1, keepdims=True) * (sections * rows) / safe
    row_weight = jnp.sum(belongs * weight, axis=1, keepdims=True)
    grad_ref[...] = (row_weight * difference).astype(BF16)
    loss_ref[...] = group_loss[:, 0:GROUPS]


def per_device(
    slots, sent, per_group, tokens, targets, group_ids, expert_ids, norm_gain, router, w_gate, w_up, w_down
):
    sections = lax.axis_size("section")
    experts = lax.axis_size("expert")
    chips = experts * 2
    groups = chips // per_group
    rows = tokens.shape[1]
    width = w_gate.shape[2]
    hidden = w_gate.shape[3]
    choices = jnp.transpose(expert_ids[0, 0], (0, 2, 1))
    router_rows = jnp.transpose(router[0])
    if experts < 8:
        router_rows = jnp.zeros((8, LANES), BF16).at[:experts].set(router_rows)
    vmem = pl.BlockSpec(memory_space=pltpu.VMEM)
    anywhere = pl.BlockSpec(memory_space=pl.ANY)
    dma = pltpu.SemaphoreType.DMA
    scratch = [
        pltpu.VMEM((2, chips, LANES, 2 * hidden), BF16),
        pltpu.VMEM((2, chips, hidden, LANES), BF16),
        pltpu.VMEM((sections + 1, rows, LANES), BF16),
        pltpu.VMEM((sections, rows, LANES), BF16),
        pltpu.VMEM((experts * slots, LANES), BF16),
        pltpu.VMEM((2, 2, chips, slots, LANES), BF16),
        pltpu.VMEM((slots, 2 * hidden), F32),
        pltpu.VMEM((slots, LANES), F32),
        pltpu.VMEM((slots, 16), F32),
        pltpu.VMEM((2, slots, hidden), BF16),
        pltpu.VMEM((chips // 2, slots, 2 * LANES), F32),
        pltpu.VMEM((chips, slots, LANES), BF16),
        pltpu.VMEM((sections, chips, slots, LANES), BF16),
        pltpu.VMEM((rows, LANES), BF16),
        pltpu.VMEM((1, rows), jnp.int32),
        pltpu.VMEM((sections, 2, rows), jnp.int32),
        pltpu.VMEM((sections, 2, rows), jnp.int32),
        pltpu.VMEM((1, LANES), F32),
        pltpu.VMEM((8, LANES), BF16),
        pltpu.VMEM((experts * slots, rows), BF16),
        pltpu.VMEM((rows, experts * slots), BF16),
        pltpu.VMEM((16, rows), BF16),
        pltpu.VMEM((rows, rows), BF16),
        pltpu.VMEM((rows, rows), BF16),
        pltpu.VMEM((16, LANES), F32),
        pltpu.VMEM((2, chips, 16, LANES), F32),
        pltpu.VMEM((2, 16, chips * LANES), BF16),
        pltpu.VMEM((2, 8, LANES), F32),
        pltpu.VMEM((chips, 8, LANES), F32),
        pltpu.VMEM((2, sections, 8, LANES), F32),
        dma((6,)),
        dma((4,)),
        dma((chips,)),
        dma((chips,)),
        dma((chips,)),
        dma((chips,)),
        dma((2, chips)),
        dma((groups,)),
        dma((2, groups)),
        dma((1,)),
        dma((1,)),
        dma((chips,)),
        dma((sections,)),
        dma((1,)),
        dma((sections,)),
        dma((chips,)),
        dma((chips,)),
        dma((1,)),
        dma((1,)),
        dma((1,)),
        dma((1,)),
        dma((chips,)),
        dma((chips,)),
        dma((2 * sections - 1,)),
        dma((2 * sections - 1,)),
    ]
    grad, loss = pl.pallas_call(
        functools.partial(kernel, sections, experts, slots, sent, per_group, float(width)),
        out_shape=(
            jax.ShapeDtypeStruct((rows, LANES), BF16),
            jax.ShapeDtypeStruct((1, GROUPS), F32),
        ),
        in_specs=[anywhere] * 9,
        out_specs=(vmem, vmem),
        scratch_shapes=scratch,
        compiler_params=pltpu.CompilerParams(
            collective_id=0, has_side_effects=True, vmem_limit_bytes=60 * 1024 * 1024
        ),
        name="moe_ring",
    )(
        tokens[0],
        targets[0],
        group_ids,
        choices,
        norm_gain,
        router_rows,
        w_gate.reshape(chips, 2, LANES, hidden),
        w_up.reshape(chips, 2, LANES, hidden),
        w_down.reshape(hidden, width),
    )
    return grad[None], loss[0]


def build(mesh, slots, sent, per_group):
    placed = (
        P("section", None, ("expert", "dp")),
        P("section", None, ("expert", "dp")),
        P("section", None),
        P(None, "section", None, None, None),
        P("section", ("expert", "dp")),
        P("section", ("expert", "dp"), None),
        P("section", "expert", None, "dp"),
        P("section", "expert", None, "dp"),
        P("section", "expert", "dp", None),
    )
    return jax.shard_map(
        functools.partial(per_device, slots, sent, per_group),
        mesh=mesh,
        in_specs=placed,
        out_specs=(P("section", None, ("expert", "dp")), P()),
        check_vma=False,
    )


def solution(mesh):
    return build(mesh, 80, 72, 4)
```

```python
import functools

import jax
import jax.numpy as jnp
from jax import lax
from jax.experimental import pallas as pl
from jax.experimental.pallas import tpu as pltpu
from jax.sharding import PartitionSpec as P

MESH = pl.DeviceIdType.MESH
GROUPS = 8
TOPK = 2
DRO_RATE = 0.3
LANES = 128
F32 = jnp.float32
BF16 = jnp.bfloat16
LAST_DIMS = (((1,), (1,)), ((), ()))


def dot(a, b):
    return jnp.dot(a, b, preferred_element_type=F32)


def dot_t(a, b):
    return lax.dot_general(a, b, LAST_DIMS, preferred_element_type=F32)


def ones_where(mask):
    return jnp.where(mask, 1.0, 0.0).astype(BF16)


def kernel(
    sections, experts, slots, sent, per_group, width,
    tok_ref, tgt_ref, gid_ref, ids_ref, gain_ref, rt_ref, wg_ref, wu_ref, wd_ref,
    grad_ref, loss_ref,
    w_gu, w_dn, x_all, x_res, out_buf, x_in, acc, sq_acc, logit_acc, act, dn_acc, part_out, part_in,
    tgt, gid, ids, gain_row, rt_raw, tgt_near, gid_near, ids_near, gain_near, ids_out, ids_back, gain_out, x_last,
    pick, scat, chosen_mask, upper, eye, rt_mine, rt_in, rt_bf, red_mine, red_in, red_z,
    in_sem, w_sem, wd_sem, wd_send, wd_recv, d_send, d_recv, f_send, f_recv, a_send, a_recv,
    c_send, c_recv, c_own, z_send, z_recv, r_send, r_recv, rf_send, rf_recv, n_send, n_recv, s_send, s_recv,
    sz_send, sz_recv, l_send, l_recv,
):
    chips = experts * 2
    across = 4
    down = chips // across
    rows = tok_ref.shape[0]
    hidden = wg_ref.shape[-1]
    section = lax.axis_index("section")
    expert = lax.axis_index("expert")
    lane = lax.axis_index("dp")
    core = lax.rem(lane, 2)
    half = lane // 2
    x_place = lax.rem(expert, across)
    y_place = expert // across * 2 + half
    mine = expert * 2 + half
    other = 1 - core
    sibling = (section, expert, half * 2 + other)

    def hops(offset):
        return min(offset[0], across - offset[0]) + min(offset[1], down - offset[1])

    offsets = [(dx, dy) for dx in range(across) for dy in range(down)]
    order = [(0, 0)] + sorted(offsets[1:], key=lambda offset: -hops(offset))
    sends = order[1:] + order[:1]

    def chip(offset, sign=1):
        x = lax.rem(x_place + across + sign * offset[0], across)
        y = lax.rem(y_place + down + sign * offset[1], down)
        return y // 2 * across + x, lax.rem(y, 2)

    def place_of(offset, sign=1):
        e, h = chip(offset, sign)
        return e * 2 + h

    def device(offset, on=0, swap=0):
        e, h = chip(offset)
        return (lax.rem(section + on, sections), e, h * 2 + (other if swap else core))

    def remote(src, dst, send, recv, target):
        return pltpu.make_async_remote_copy(
            src_ref=src, dst_ref=dst, send_sem=send, recv_sem=recv, device_id=target, device_id_type=MESH
        )

    inputs = [
        pltpu.make_async_copy(src, dst, in_sem.at[n])
        for n, (src, dst) in enumerate(
            [(ids_ref, ids), (tok_ref, x_all.at[0]), (gain_ref, gain_row), (rt_ref, rt_raw), (tgt_ref, tgt), (gid_ref, gid)]
        )
    ]
    loads = []
    for side in range(2):
        loads.append(pltpu.make_async_copy(wg_ref.at[:, side], w_gu.at[side, :, :, 0:hidden], w_sem.at[2 * side]))
        loads.append(
            pltpu.make_async_copy(wu_ref.at[:, side], w_gu.at[side, :, :, hidden : 2 * hidden], w_sem.at[2 * side + 1])
        )
    for j in range(chips):
        own_columns = pl.ds(pl.multiple_of(j * 2 * LANES + core * LANES, LANES), LANES)
        loads.append(pltpu.make_async_copy(wd_ref.at[:, own_columns], w_dn.at[core, j], wd_sem.at[j]))
    for load in inputs + loads:
        load.start()

    part_in[...] = jnp.zeros(part_in.shape, BF16)

    barrier = pltpu.get_barrier_semaphore()
    partners = {(dx, dy, 0, 0) for dx, dy in offsets[1:]} | {(0, 0, 0, 1)}
    partners |= {(dx, dy, dz % sections, 0) for dx, dy in offsets for dz in (1, -1)}
    partners |= {(0, 0, dz, swap) for dz in range(1, sections) for swap in range(2)}
    for dx, dy, dz, swap in sorted(partners):
        pl.semaphore_signal(barrier, inc=1, device_id=device((dx, dy), dz, swap), device_id_type=MESH)

    first = lax.broadcasted_iota(jnp.int32, (rows, rows), 0)
    second = lax.broadcasted_iota(jnp.int32, (rows, rows), 1)
    upper[...] = ones_where(first < second)
    eye[...] = ones_where(first == second)
    for load in inputs:
        load.wait()
    gain = gain_row[...]
    rt_mine[0:8, :] = rt_raw[...].astype(F32)
    rt_mine[8:16, :] = jnp.broadcast_to(1.0 / (gain * gain), (8, LANES))
    rt_in[core, 0] = rt_mine[...]
    gain_out[...] = gain

    expert_rows = lax.broadcasted_iota(jnp.int32, (16, rows), 0)

    slot_rows = lax.broadcasted_iota(jnp.int32, (slots, rows), 0).astype(F32)

    def micro_of(place):
        return lax.rem(place + 2 * sections, sections)

    def ranks(table, micro):
        first_id = table[micro, 0:1, :]
        second_id = table[micro, 1:2, :]
        hit_first = first_id == expert_rows
        hit_second = second_id == expert_rows
        either = hit_first | hit_second
        named = ones_where(either)
        return first_id, second_id, hit_first, hit_second, either, named, dot(named, upper[...])

    def prepare_pick(table, micro):
        _, _, _, _, either, _, rank = ranks(table, micro)
        key = jnp.where(either, rank, -1.0)
        for e in range(experts):
            pick[e * slots : (e + 1) * slots, :] = ones_where(key[e : e + 1, :] == slot_rows)

    def prepare_mask(moment):
        _, _, _, _, either, named, rank = ranks(ids, micro_of(section - moment))
        key = jnp.sum(jnp.where(expert_rows == expert, jnp.where(either, rank, -1.0), 0.0), axis=0, keepdims=True)
        chosen_mask[...] = dot_t(ones_where(key == slot_rows), named)

    def prepare_scatter(moment):
        first_id, second_id, hit_first, hit_second, _, _, rank = ranks(
            ids_back, micro_of(section + core - 1 - moment)
        )
        rank_first = jnp.sum(jnp.where(hit_first, rank, 0.0), axis=0, keepdims=True)
        rank_second = jnp.sum(jnp.where(hit_second, rank, 0.0), axis=0, keepdims=True)
        table = jnp.where(expert_rows == 0, first_id.astype(F32), second_id.astype(F32))
        table = jnp.where(expert_rows == 2, rank_first, table)
        table = jnp.where(expert_rows == 3, rank_second, table)
        spread = dot_t(eye[...], table.astype(BF16))
        slot_first = spread[:, 0:1] * slots + spread[:, 2:3]
        slot_second = spread[:, 1:2] * slots + spread[:, 3:4]
        lanes = lax.broadcasted_iota(jnp.int32, (rows, LANES), 1).astype(F32)
        for n in range(experts * slots // LANES):
            here = lanes + float(n * LANES)
            scat[:, n * LANES : (n + 1) * LANES] = ones_where((slot_first == here) | (slot_second == here))

    prepare_pick(ids, section)

    pl.semaphore_wait(barrier, len(partners))

    def router_copy(k):
        return remote(rt_mine, rt_in.at[core, k], r_send.at[k], r_recv.at[k], device(order[k]))

    toward = device((0, 0), sections + 1 - 2 * core)
    neighbour = [
        remote(src, dst, n_send.at[n], n_recv.at[n], toward)
        for n, (src, dst) in enumerate([(ids, ids_near), (gain_row, gain_near), (gid, gid_near), (tgt, tgt_near)])
    ]

    def down_copy(j):
        sib_columns = pl.ds(pl.multiple_of(j * 2 * LANES + other * LANES, LANES), LANES)
        return remote(wd_ref.at[:, sib_columns], w_dn.at[core, j], wd_send.at[j], wd_recv.at[j], sibling)

    for k in range(1, chips):
        router_copy(k).start()
    for copy in neighbour:
        copy.start()

    def begun(moment):
        return 1 - (sections - moment) // sections

    def stays(moment):
        return core * begun(moment) == 0

    def dispatch_copy(k, moment):
        e, _ = chip(order[k])
        block = pl.ds(pl.multiple_of(e * slots, 16), sent)
        return remote(
            out_buf.at[block, :], x_in.at[moment, core, k, pl.ds(0, sent)], d_send.at[k], d_recv.at[moment, k],
            device(order[k], core * begun(moment)),
        )

    def dispatch(moment):
        scaled = (x_all[moment].astype(F32) * gain_out[...]).astype(BF16)
        out_buf[...] = dot(pick[...], scaled).astype(BF16)
        for k in range(1, chips):
            dispatch_copy(k, moment).start()

        @pl.when(stays(moment))
        def _():
            x_in[moment, core, 0] = out_buf[pl.ds(pl.multiple_of(expert * slots, 16), slots), :]

        @pl.when(jnp.logical_not(stays(moment)))
        def _():
            dispatch_copy(0, moment).start()

    def first_tick():
        for j in range(chips):
            down_copy(j).start()
        for k in range(1, chips):
            copy = router_copy(k)
            copy.wait_recv()
            copy.wait_send()
        forward = remote(rt_in.at[core], rt_in.at[core], rf_send.at[0], rf_recv.at[0], sibling)
        forward.start()
        for copy in neighbour:
            copy.wait_recv()
            copy.wait_send()
        ids_out[...] = jnp.where(core == 0, ids[...], ids_near[...])
        ids_back[...] = jnp.where(core == 0, ids_near[...], ids[...])
        gain_out[...] = jnp.where(core == 0, gain_row[...], gain_near[...])
        forward.wait_send()
        remote(rt_in.at[other], rt_in.at[other], rf_send.at[0], rf_recv.at[0], sibling).wait_recv()
        for side in range(2):
            for k in range(chips):
                rt_bf[side, :, k * LANES : (k + 1) * LANES] = rt_in[side, k].astype(BF16)
        for load in loads:
            load.wait()

    def down_here():
        for j in range(chips):
            copy = remote(wd_ref.at[:, pl.ds(0, LANES)], w_dn.at[other, j], wd_send.at[j], wd_recv.at[j], sibling)
            copy.wait_send()
            copy.wait_recv()

    group_count = chips // per_group

    def group_work(moment, source, g, fresh):
        ks = range(g * per_group, (g + 1) * per_group)
        blocks = [x_in[moment, source, k] for k in ks]
        block = jnp.concatenate(blocks, axis=1)
        weight = jnp.concatenate([w_gu[source, place_of(order[k], -1)] for k in ks], axis=0)
        product = dot(block, weight)
        router = rt_bf[source, :, g * per_group * LANES : (g + 1) * per_group * LANES]
        logits = dot_t(block, router)
        squares = None
        for k, piece in zip(ks, blocks):
            wide = piece.astype(F32)
            term = wide * wide * rt_in[source, k, 8:9, :]
            squares = term if squares is None else squares + term
        if fresh:
            acc[...] = product
            logit_acc[...] = logits
            sq_acc[...] = squares
        else:
            acc[...] += product
            logit_acc[...] += logits
            sq_acc[...] += squares

    def forward_copy(source, g, moment):
        block = x_in.at[moment, source, pl.ds(g * per_group, per_group)]
        return remote(block, block, f_send.at[g], f_recv.at[g], sibling)

    def own_group(g, moment, fresh=False):
        if g == 0:

            @pl.when(jnp.logical_not(stays(moment)))
            def _():
                dispatch_copy(0, moment).wait_recv()

        for k in range(max(1, g * per_group), (g + 1) * per_group):
            dispatch_copy(k, moment).wait_recv()
        forward_copy(core, g, moment).start()
        group_work(moment, core, g, fresh)

    def sibling_group(g, moment):
        forward_copy(other, g, moment).wait_recv()
        group_work(moment, other, g, False)

    pairs = [(n, n + 1) for n in range(0, chips, 2)]

    def tick(moment, carry):
        dispatch(moment)
        ahead = remote(
            x_all.at[moment], x_res.at[moment], z_send.at[0], z_recv.at[moment], device((0, 0), 1)
        )
        ahead.start()

        @pl.when(moment == 0)
        def _():
            first_tick()

        prepare_mask(moment)
        prepare_scatter(moment)

        own_group(0, moment, True)
        for g in range(1, group_count):
            own_group(g, moment)
            sibling_group(g - 1, moment)
        sibling_group(group_count - 1, moment)

        row_scale = lax.rsqrt(jnp.sum(sq_acc[...], axis=1, keepdims=True) / width + 1e-6)
        gate_part = acc[:, 0:hidden] * row_scale
        up_part = acc[:, hidden : 2 * hidden] * row_scale
        act[core] = (gate_part / (1.0 + jnp.exp(-gate_part)) * up_part).astype(BF16)
        swap = remote(act.at[core], act.at[core], a_send.at[0], a_recv.at[0], sibling)
        swap.start()

        chosen = chosen_mask[...] > 0.5
        logits = logit_acc[...] * row_scale
        lanes = lax.broadcasted_iota(jnp.int32, (slots, 16), 1)
        top = jnp.max(jnp.where(chosen, logits, -1e30), axis=1, keepdims=True)
        raised = jnp.where(chosen, jnp.exp(jnp.where(chosen, logits - top, 0.0)), 0.0)
        gate = jnp.sum(jnp.where(lanes == expert, raised, 0.0), axis=1, keepdims=True) / jnp.maximum(
            jnp.sum(raised, axis=1, keepdims=True), 1e-30
        )

        def down_weight(source, pair):
            return jnp.concatenate([w_dn[source, place_of(sends[n])] for n in pair], axis=1)

        own_act = act[core]
        for i, pair in enumerate(pairs):
            dn_acc[i] = dot(own_act, down_weight(core, pair))
        for g in range(group_count):
            forward_copy(core, g, moment).wait_send()
        for k in range(1, chips):
            dispatch_copy(k, moment).wait_send()

        @pl.when(jnp.logical_not(stays(moment)))
        def _():
            dispatch_copy(0, moment).wait_send()

        @pl.when(moment == 0)
        def _():
            down_here()

        remote(act.at[other], act.at[other], a_send.at[0], a_recv.at[0], sibling).wait_recv()
        swap.wait_send()
        sib_act = act[other]
        landing = half * experts + expert

        def part_copy(n):
            return remote(
                part_out.at[n, pl.ds(0, sent)], part_in.at[moment, landing, pl.ds(0, sent)], c_send.at[n],
                c_own.at[moment] if n == chips - 1 else c_recv.at[moment], device(sends[n], 1 - core),
            )

        for i, pair in enumerate(pairs):
            piece = ((dn_acc[i] + dot(sib_act, down_weight(other, pair))) * gate).astype(BF16)
            for at, n in enumerate(pair):
                value = piece[:, at * LANES : (at + 1) * LANES]
                part_out[n] = value
                if n < chips - 1:
                    part_copy(n).start()
                else:

                    @pl.when(core == 0)
                    def _(n=n):
                        part_copy(n).start()

                    @pl.when(core == 1)
                    def _(value=value):
                        part_in[moment, landing, 0:sent, :] = value[0:sent, :]

        prepare_pick(ids_out, micro_of(section + core - moment - 1))

        for n in range(chips - 1):
            part_copy(n).wait_send()

        @pl.when(core == 0)
        def _():
            part_copy(chips - 1).wait_send()
            part_copy(chips - 1).wait_recv()

        ahead.wait_send()
        ahead.wait_recv()
        everything = part_in.at[moment, pl.ds(0, chips - 1), pl.ds(0, sent)]
        remote(everything, everything, c_send.at[0], c_recv.at[moment], device((0, 0), 1)).wait_recv()
        table = scat[...]
        count = experts * slots
        parts = part_in[moment].reshape(chips * slots, LANES)
        moe = dot(table, parts[0:count]) + dot(table, parts[count : 2 * count])
        kept = jnp.where(core * (1 - begun(moment)) == 1, x_all[0].astype(F32), x_res[moment].astype(F32))
        x_all[moment + 1] = (kept + moe).astype(BF16)
        return carry

    lax.fori_loop(0, sections, tick, 0)

    last = remote(x_all.at[sections], x_last, l_send.at[0], l_recv.at[0], device((0, 0), 1))
    last.start()
    lanes = lax.broadcasted_iota(jnp.int32, (rows, LANES), 1).astype(F32)

    def members(group_row):
        column = dot_t(eye[...], jnp.broadcast_to(group_row.astype(F32), (16, rows)).astype(BF16))[:, 0:1]
        return jnp.where(column == lanes, 1.0, 0.0)

    aim = jnp.where(core == 0, tgt[...].astype(F32), tgt_near[...].astype(F32))
    error = x_all[sections].astype(F32) - aim
    row_loss = jnp.sum(error * error, axis=1, keepdims=True) / width
    belongs = members(jnp.where(core == 0, gid[...], gid_near[...]))
    totals = jnp.sum(belongs * row_loss, axis=0, keepdims=True)
    counts = jnp.sum(belongs, axis=0, keepdims=True)
    red_rows = lax.broadcasted_iota(jnp.int32, (8, LANES), 0)
    local = jnp.where(red_rows == 0, totals, counts)
    red_mine[0] = local
    red_in[mine] = local

    def plane_copy(k, place):
        return remote(red_mine.at[0], red_in.at[place], s_send.at[k], s_recv.at[k], device(order[k]))

    for k in range(1, chips):
        plane_copy(k, mine).start()
    for k in range(1, chips):
        copy = plane_copy(k, place_of(order[k], -1))
        copy.wait_recv()
        copy.wait_send()
    plane = red_in[0]
    for j in range(1, chips):
        plane = plane + red_in[j]
    red_mine[1] = plane
    red_z[core, section] = plane
    steps = [(dz, swap) for dz in range(sections) for swap in range(2) if dz or swap]

    def depth_copy(n, lane_core, place):
        dz, swap = steps[n]
        return remote(
            red_mine.at[1], red_z.at[lane_core, place], sz_send.at[n], sz_recv.at[n], device((0, 0), dz, swap)
        )

    for n in range(len(steps)):
        depth_copy(n, core, section).start()
    for n, (dz, swap) in enumerate(steps):
        copy = depth_copy(n, other if swap else core, lax.rem(section + sections - dz, sections))
        copy.wait_recv()
        copy.wait_send()
    whole = red_z[0, 0]
    for n in range(1, 2 * sections):
        whole = whole + red_z[n // sections, n % sections]
    total = whole[0:1, :]
    count = whole[1:2, :] / (chips * 2)
    safe = jnp.maximum(count, 1.0)
    group_loss = total / safe
    lane_row = lax.broadcasted_iota(jnp.int32, (1, LANES), 1)
    raised = jnp.where(lane_row < GROUPS, jnp.exp(DRO_RATE * group_loss), 0.0)
    weight = raised / jnp.sum(raised, axis=1, keepdims=True) * (sections * rows) / safe
    row_weight = jnp.sum(members(gid[...]) * weight, axis=1, keepdims=True)
    last.wait_send()
    last.wait_recv()
    final = jnp.where(core == 0, x_all[sections].astype(F32), x_last[...].astype(F32))
    difference = final - tgt[...].astype(F32)
    grad_ref[...] = (row_weight * difference).astype(BF16)
    loss_ref[...] = group_loss[:, 0:GROUPS]


def per_device(
    slots, sent, per_group, tokens, targets, group_ids, expert_ids, norm_gain, router, w_gate, w_up, w_down
):
    sections = lax.axis_size("section")
    experts = lax.axis_size("expert")
    chips = experts * 2
    groups = chips // per_group
    rows = tokens.shape[1]
    width = w_gate.shape[2]
    hidden = w_gate.shape[3]
    choices = jnp.transpose(expert_ids[0, 0], (0, 2, 1))
    router_rows = jnp.transpose(router[0])
    if experts < 8:
        router_rows = jnp.zeros((8, LANES), BF16).at[:experts].set(router_rows)
    vmem = pl.BlockSpec(memory_space=pltpu.VMEM)
    anywhere = pl.BlockSpec(memory_space=pl.ANY)
    dma = pltpu.SemaphoreType.DMA
    scratch = [
        pltpu.VMEM((2, chips, LANES, 2 * hidden), BF16),
        pltpu.VMEM((2, chips, hidden, LANES), BF16),
        pltpu.VMEM((sections + 1, rows, LANES), BF16),
        pltpu.VMEM((sections, rows, LANES), BF16),
        pltpu.VMEM((experts * slots, LANES), BF16),
        pltpu.VMEM((sections, 2, chips, slots, LANES), BF16),
        pltpu.VMEM((slots, 2 * hidden), F32),
        pltpu.VMEM((slots, LANES), F32),
        pltpu.VMEM((slots, 16), F32),
        pltpu.VMEM((2, slots, hidden), BF16),
        pltpu.VMEM((chips // 2, slots, 2 * LANES), F32),
        pltpu.VMEM((chips, slots, LANES), BF16),
        pltpu.VMEM((sections, chips, slots, LANES), BF16),
        pltpu.VMEM((rows, LANES), BF16),
        pltpu.VMEM((1, rows), jnp.int32),
        pltpu.VMEM((sections, 2, rows), jnp.int32),
        pltpu.VMEM((1, LANES), F32),
        pltpu.VMEM((8, LANES), BF16),
        pltpu.VMEM((rows, LANES), BF16),
        pltpu.VMEM((1, rows), jnp.int32),
        pltpu.VMEM((sections, 2, rows), jnp.int32),
        pltpu.VMEM((1, LANES), F32),
        pltpu.VMEM((sections, 2, rows), jnp.int32),
        pltpu.VMEM((sections, 2, rows), jnp.int32),
        pltpu.VMEM((1, LANES), F32),
        pltpu.VMEM((rows, LANES), BF16),
        pltpu.VMEM((experts * slots, rows), BF16),
        pltpu.VMEM((rows, experts * slots), BF16),
        pltpu.VMEM((slots, 16), F32),
        pltpu.VMEM((rows, rows), BF16),
        pltpu.VMEM((rows, rows), BF16),
        pltpu.VMEM((16, LANES), F32),
        pltpu.VMEM((2, chips, 16, LANES), F32),
        pltpu.VMEM((2, 16, chips * LANES), BF16),
        pltpu.VMEM((2, 8, LANES), F32),
        pltpu.VMEM((chips, 8, LANES), F32),
        pltpu.VMEM((2, sections, 8, LANES), F32),
        dma((6,)),
        dma((4,)),
        dma((chips,)),
        dma((chips,)),
        dma((chips,)),
        dma((chips,)),
        dma((sections, chips)),
        dma((groups,)),
        dma((groups,)),
        dma((1,)),
        dma((1,)),
        dma((chips,)),
        dma((sections,)),
        dma((sections,)),
        dma((1,)),
        dma((sections,)),
        dma((chips,)),
        dma((chips,)),
        dma((1,)),
        dma((1,)),
        dma((4,)),
        dma((4,)),
        dma((chips,)),
        dma((chips,)),
        dma((2 * sections - 1,)),
        dma((2 * sections - 1,)),
        dma((1,)),
        dma((1,)),
    ]
    grad, loss = pl.pallas_call(
        functools.partial(kernel, sections, experts, slots, sent, per_group, float(width)),
        out_shape=(
            jax.ShapeDtypeStruct((rows, LANES), BF16),
            jax.ShapeDtypeStruct((1, GROUPS), F32),
        ),
        in_specs=[anywhere] * 9,
        out_specs=(vmem, vmem),
        scratch_shapes=scratch,
        compiler_params=pltpu.CompilerParams(
            collective_id=0, has_side_effects=True, vmem_limit_bytes=60 * 1024 * 1024
        ),
        name="moe_ring",
    )(
        tokens[0],
        targets[0],
        group_ids,
        choices,
        norm_gain,
        router_rows,
        w_gate.reshape(chips, 2, LANES, hidden),
        w_up.reshape(chips, 2, LANES, hidden),
        w_down.reshape(hidden, width),
    )
    return grad[None], loss[0]


def build(mesh, slots, sent, per_group):
    placed = (
        P("section", None, ("expert", "dp")),
        P("section", None, ("expert", "dp")),
        P("section", None),
        P(None, "section", None, None, None),
        P("section", ("expert", "dp")),
        P("section", ("expert", "dp"), None),
        P("section", "expert", None, "dp"),
        P("section", "expert", None, "dp"),
        P("section", "expert", "dp", None),
    )
    return jax.shard_map(
        functools.partial(per_device, slots, sent, per_group),
        mesh=mesh,
        in_specs=placed,
        out_specs=(P("section", None, ("expert", "dp")), P()),
        check_vma=False,
    )


def solution(mesh):
    return build(mesh, 80, 72, 4)
```

```python
import functools

import jax
import jax.numpy as jnp
from jax import lax
from jax.experimental import pallas as pl
from jax.experimental.pallas import tpu as pltpu
from jax.sharding import PartitionSpec as P

MESH = pl.DeviceIdType.MESH
GROUPS = 8
TOPK = 2
DRO_RATE = 0.3
LANES = 128
F32 = jnp.float32
BF16 = jnp.bfloat16
LAST_DIMS = (((1,), (1,)), ((), ()))


def dot(a, b):
    return jnp.dot(a, b, preferred_element_type=F32)


def dot_t(a, b):
    return lax.dot_general(a, b, LAST_DIMS, preferred_element_type=F32)


def ones_where(mask):
    return jnp.where(mask, 1.0, 0.0).astype(BF16)


def kernel(
    sections, experts, slots, sent, groups, spread_out, width,
    tok_ref, tgt_ref, gid_ref, ids_ref, gain_ref, rt_ref, wg_ref, wu_ref, wd_ref,
    grad_ref, loss_ref,
    w_gu, w_dn, x_all, x_res, out_buf, x_in, acc, sq_acc, logit_acc, act, dn_acc, part_out, part_in,
    tgt, gid, ids, gain_row, rt_raw, tgt_near, gid_near, ids_near, gain_near, ids_out, ids_back, gain_out, x_last,
    pick, scat, chosen_mask, upper, eye, rt_mine, rt_in, rt_bf, red_mine, red_in, red_z,
    in_sem, w_sem, wd_sem, wd_send, wd_recv, d_send, d_recv, f_send, f_recv, a_send, a_recv,
    c_send, c_recv, c_own, z_send, z_recv, r_send, r_recv, rf_send, rf_recv, n_send, n_recv, s_send, s_recv,
    sz_send, sz_recv, l_send, l_recv,
):
    chips = experts * 2
    across = 4
    down = chips // across
    rows = tok_ref.shape[0]
    hidden = wg_ref.shape[-1]
    section = lax.axis_index("section")
    expert = lax.axis_index("expert")
    lane = lax.axis_index("dp")
    core = lax.rem(lane, 2)
    half = lane // 2
    x_place = lax.rem(expert, across)
    y_place = expert // across * 2 + half
    mine = expert * 2 + half
    other = 1 - core
    sibling = (section, expert, half * 2 + other)

    def hops(offset):
        return min(offset[0], across - offset[0]) + min(offset[1], down - offset[1])

    offsets = [(dx, dy) for dx in range(across) for dy in range(down)]
    order = [(0, 0)] + sorted(offsets[1:], key=lambda offset: -hops(offset))
    sends = order[1:] + order[:1]

    def chip(offset, sign=1):
        x = lax.rem(x_place + across + sign * offset[0], across)
        y = lax.rem(y_place + down + sign * offset[1], down)
        return y // 2 * across + x, lax.rem(y, 2)

    def place_of(offset, sign=1):
        e, h = chip(offset, sign)
        return e * 2 + h

    def device(offset, on=0, swap=0):
        e, h = chip(offset)
        return (lax.rem(section + on, sections), e, h * 2 + (other if swap else core))

    def remote(src, dst, send, recv, target):
        return pltpu.make_async_remote_copy(
            src_ref=src, dst_ref=dst, send_sem=send, recv_sem=recv, device_id=target, device_id_type=MESH
        )

    inputs = [
        pltpu.make_async_copy(src, dst, in_sem.at[n])
        for n, (src, dst) in enumerate(
            [(ids_ref, ids), (tok_ref, x_all.at[0]), (gain_ref, gain_row), (rt_ref, rt_raw), (tgt_ref, tgt), (gid_ref, gid)]
        )
    ]
    loads = []
    for side in range(2):
        loads.append(pltpu.make_async_copy(wg_ref.at[:, side], w_gu.at[side, :, :, 0:hidden], w_sem.at[2 * side]))
        loads.append(
            pltpu.make_async_copy(wu_ref.at[:, side], w_gu.at[side, :, :, hidden : 2 * hidden], w_sem.at[2 * side + 1])
        )
    for j in range(chips):
        own_columns = pl.ds(pl.multiple_of(j * 2 * LANES + core * LANES, LANES), LANES)
        loads.append(pltpu.make_async_copy(wd_ref.at[:, own_columns], w_dn.at[core, j], wd_sem.at[j]))
    for load in inputs:
        load.start()

    part_in[:, :, sent:slots, :] = jnp.zeros((sections, chips, slots - sent, LANES), BF16)

    barrier = pltpu.get_barrier_semaphore()
    partners = {(dx, dy, 0, 0) for dx, dy in offsets[1:]} | {(0, 0, 0, 1)}
    partners |= {(dx, dy, dz % sections, 0) for dx, dy in offsets for dz in (1, -1)}
    partners |= {(0, 0, dz, swap) for dz in range(1, sections) for swap in range(2)}
    for dx, dy, dz, swap in sorted(partners):
        pl.semaphore_signal(barrier, inc=1, device_id=device((dx, dy), dz, swap), device_id_type=MESH)
    for load in loads:
        load.start()

    first = lax.broadcasted_iota(jnp.int32, (rows, rows), 0)
    second = lax.broadcasted_iota(jnp.int32, (rows, rows), 1)
    upper[...] = ones_where(first < second)
    eye[...] = ones_where(first == second)
    for load in inputs:
        load.wait()
    gain = gain_row[...]
    rt_mine[0:8, :] = rt_raw[...].astype(F32)
    rt_mine[8:16, :] = jnp.broadcast_to(1.0 / (gain * gain), (8, LANES))
    rt_in[core, 0] = rt_mine[...]
    gain_out[...] = gain

    expert_rows = lax.broadcasted_iota(jnp.int32, (16, rows), 0)

    slot_rows = lax.broadcasted_iota(jnp.int32, (slots, rows), 0).astype(F32)

    def micro_of(place):
        return lax.rem(place + 2 * sections, sections)

    def ranks(table, micro):
        first_id = table[micro, 0:1, :]
        second_id = table[micro, 1:2, :]
        hit_first = first_id == expert_rows
        hit_second = second_id == expert_rows
        either = hit_first | hit_second
        named = ones_where(either)
        return first_id, second_id, hit_first, hit_second, either, named, dot(named, upper[...])

    def prepare_pick(table, micro):
        _, _, _, _, either, _, rank = ranks(table, micro)
        key = jnp.where(either, rank, -1.0)
        for e in range(experts):
            pick[e * slots : (e + 1) * slots, :] = ones_where(key[e : e + 1, :] == slot_rows)

    def prepare_mask(moment):
        _, _, _, _, either, named, rank = ranks(ids, micro_of(section - moment))
        key = jnp.sum(jnp.where(expert_rows == expert, jnp.where(either, rank, -1.0), 0.0), axis=0, keepdims=True)
        chosen_mask[...] = dot_t(ones_where(key == slot_rows), named)

    def prepare_scatter(moment):
        first_id, second_id, hit_first, hit_second, _, _, rank = ranks(
            ids_back, micro_of(section + core - 1 - moment)
        )
        rank_first = jnp.sum(jnp.where(hit_first, rank, 0.0), axis=0, keepdims=True)
        rank_second = jnp.sum(jnp.where(hit_second, rank, 0.0), axis=0, keepdims=True)
        table = jnp.where(expert_rows == 0, first_id.astype(F32), second_id.astype(F32))
        table = jnp.where(expert_rows == 2, rank_first, table)
        table = jnp.where(expert_rows == 3, rank_second, table)
        spread = dot_t(eye[...], table.astype(BF16))
        slot_first = spread[:, 0:1] * slots + spread[:, 2:3]
        slot_second = spread[:, 1:2] * slots + spread[:, 3:4]
        lanes = lax.broadcasted_iota(jnp.int32, (rows, LANES), 1).astype(F32)
        for n in range(experts * slots // LANES):
            here = lanes + float(n * LANES)
            scat[:, n * LANES : (n + 1) * LANES] = ones_where((slot_first == here) | (slot_second == here))

    prepare_pick(ids, section)

    pl.semaphore_wait(barrier, len(partners))

    def router_copy(k):
        return remote(rt_mine, rt_in.at[core, k], r_send.at[k], r_recv.at[k], device(order[k]))

    toward = device((0, 0), sections + 1 - 2 * core)
    neighbour = [
        remote(src, dst, n_send.at[n], n_recv.at[n], toward)
        for n, (src, dst) in enumerate([(ids, ids_near), (gain_row, gain_near), (gid, gid_near), (tgt, tgt_near)])
    ]

    def down_copy(j):
        sib_columns = pl.ds(pl.multiple_of(j * 2 * LANES + other * LANES, LANES), LANES)
        return remote(wd_ref.at[:, sib_columns], w_dn.at[core, j], wd_send.at[j], wd_recv.at[j], sibling)

    for k in range(1, chips):
        router_copy(k).start()
    for copy in neighbour:
        copy.start()

    def begun(moment):
        return 1 - (sections - moment) // sections

    def stays(moment):
        return core * begun(moment) == 0

    def dispatch_copy(k, moment):
        e, _ = chip(order[k])
        block = pl.ds(pl.multiple_of(e * slots, 16), sent)
        return remote(
            out_buf.at[block, :], x_in.at[moment, core, k, pl.ds(0, sent)], d_send.at[k], d_recv.at[moment, k],
            device(order[k], core * begun(moment)),
        )

    def dispatch(moment):
        scaled = (x_all[moment].astype(F32) * gain_out[...]).astype(BF16)
        out_buf[...] = dot(pick[...], scaled).astype(BF16)
        for k in range(1, chips):
            dispatch_copy(k, moment).start()

        @pl.when(stays(moment))
        def _():
            x_in[moment, core, 0] = out_buf[pl.ds(pl.multiple_of(expert * slots, 16), slots), :]

        @pl.when(jnp.logical_not(stays(moment)))
        def _():
            dispatch_copy(0, moment).start()

    def first_tick():
        for j in range(chips):
            down_copy(j).start()
        for k in range(1, chips):
            copy = router_copy(k)
            copy.wait_recv()
            copy.wait_send()
        forward = remote(rt_in.at[core], rt_in.at[core], rf_send.at[0], rf_recv.at[0], sibling)
        forward.start()
        for copy in neighbour:
            copy.wait_recv()
            copy.wait_send()
        ids_out[...] = jnp.where(core == 0, ids[...], ids_near[...])
        ids_back[...] = jnp.where(core == 0, ids_near[...], ids[...])
        gain_out[...] = jnp.where(core == 0, gain_row[...], gain_near[...])
        forward.wait_send()
        remote(rt_in.at[other], rt_in.at[other], rf_send.at[0], rf_recv.at[0], sibling).wait_recv()
        for side in range(2):
            for k in range(chips):
                rt_bf[side, :, k * LANES : (k + 1) * LANES] = rt_in[side, k].astype(BF16)
        for load in loads:
            load.wait()

    def down_here():
        for j in range(chips):
            copy = remote(wd_ref.at[:, pl.ds(0, LANES)], w_dn.at[other, j], wd_send.at[j], wd_recv.at[j], sibling)
            copy.wait_send()
            copy.wait_recv()

    group_count = len(groups)

    def group_work(moment, source, g, fresh):
        start, stop = groups[g]
        ks = range(start, stop)
        blocks = [x_in[moment, source, k] for k in ks]
        block = jnp.concatenate(blocks, axis=1)
        weight = jnp.concatenate([w_gu[source, place_of(order[k], -1)] for k in ks], axis=0)
        product = dot(block, weight)
        router = rt_bf[source, :, start * LANES : stop * LANES]
        logits = dot_t(block, router)
        squares = None
        for k, piece in zip(ks, blocks):
            wide = piece.astype(F32)
            term = wide * wide * rt_in[source, k, 8:9, :]
            squares = term if squares is None else squares + term
        if fresh:
            acc[...] = product
            logit_acc[...] = logits
            sq_acc[...] = squares
        else:
            acc[...] += product
            logit_acc[...] += logits
            sq_acc[...] += squares

    def forward_copy(source, g, moment):
        block = x_in.at[moment, source, pl.ds(groups[g][0], groups[g][1] - groups[g][0])]
        return remote(block, block, f_send.at[g], f_recv.at[g], sibling)

    def own_group(g, moment, fresh=False):
        if g == 0:

            @pl.when(jnp.logical_not(stays(moment)))
            def _():
                dispatch_copy(0, moment).wait_recv()

        for k in range(max(1, groups[g][0]), groups[g][1]):
            dispatch_copy(k, moment).wait_recv()
        forward_copy(core, g, moment).start()
        group_work(moment, core, g, fresh)

    def sibling_group(g, moment):
        forward_copy(other, g, moment).wait_recv()
        group_work(moment, other, g, False)

    pairs = [tuple(range(n, n + spread_out)) for n in range(0, chips, spread_out)]

    def tick(moment, carry):
        dispatch(moment)
        ahead = remote(
            x_all.at[moment], x_res.at[moment], z_send.at[0], z_recv.at[moment], device((0, 0), 1)
        )
        ahead.start()

        @pl.when(moment == 0)
        def _():
            first_tick()

        prepare_mask(moment)
        prepare_scatter(moment)

        own_group(0, moment, True)
        for g in range(1, group_count):
            own_group(g, moment)
            sibling_group(g - 1, moment)
        sibling_group(group_count - 1, moment)

        row_scale = lax.rsqrt(jnp.sum(sq_acc[...], axis=1, keepdims=True) / width + 1e-6)
        gate_part = acc[:, 0:hidden] * row_scale
        up_part = acc[:, hidden : 2 * hidden] * row_scale
        act[core] = (gate_part / (1.0 + jnp.exp(-gate_part)) * up_part).astype(BF16)
        swap = remote(act.at[core], act.at[core], a_send.at[0], a_recv.at[0], sibling)
        swap.start()

        chosen = chosen_mask[...] > 0.5
        logits = logit_acc[...] * row_scale
        lanes = lax.broadcasted_iota(jnp.int32, (slots, 16), 1)
        top = jnp.max(jnp.where(chosen, logits, -1e30), axis=1, keepdims=True)
        raised = jnp.where(chosen, jnp.exp(jnp.where(chosen, logits - top, 0.0)), 0.0)
        gate = jnp.sum(jnp.where(lanes == expert, raised, 0.0), axis=1, keepdims=True) / jnp.maximum(
            jnp.sum(raised, axis=1, keepdims=True), 1e-30
        )

        def down_weight(source, pair):
            return jnp.concatenate([w_dn[source, place_of(sends[n])] for n in pair], axis=1)

        own_act = act[core]
        for i, pair in enumerate(pairs):
            dn_acc[i] = dot(own_act, down_weight(core, pair))
        for g in range(group_count):
            forward_copy(core, g, moment).wait_send()
        for k in range(1, chips):
            dispatch_copy(k, moment).wait_send()

        @pl.when(jnp.logical_not(stays(moment)))
        def _():
            dispatch_copy(0, moment).wait_send()

        @pl.when(moment == 0)
        def _():
            down_here()

        remote(act.at[other], act.at[other], a_send.at[0], a_recv.at[0], sibling).wait_recv()
        swap.wait_send()
        sib_act = act[other]
        landing = half * experts + expert

        def part_copy(n):
            return remote(
                part_out.at[n, pl.ds(0, sent)], part_in.at[moment, landing, pl.ds(0, sent)], c_send.at[n],
                c_own.at[moment] if n == chips - 1 else c_recv.at[moment], device(sends[n], 1 - core),
            )

        for i, pair in enumerate(pairs):
            piece = ((dn_acc[i] + dot(sib_act, down_weight(other, pair))) * gate).astype(BF16)
            for at, n in enumerate(pair):
                value = piece[:, at * LANES : (at + 1) * LANES]
                part_out[n] = value
                if n < chips - 1:
                    part_copy(n).start()
                else:

                    @pl.when(core == 0)
                    def _(n=n):
                        part_copy(n).start()

                    @pl.when(core == 1)
                    def _(value=value):
                        part_in[moment, landing, 0:sent, :] = value[0:sent, :]

        prepare_pick(ids_out, micro_of(section + core - moment - 1))

        for n in range(chips - 1):
            part_copy(n).wait_send()

        @pl.when(core == 0)
        def _():
            part_copy(chips - 1).wait_send()
            part_copy(chips - 1).wait_recv()

        ahead.wait_send()
        ahead.wait_recv()
        everything = part_in.at[moment, pl.ds(0, chips - 1), pl.ds(0, sent)]
        remote(everything, everything, c_send.at[0], c_recv.at[moment], device((0, 0), 1)).wait_recv()
        table = scat[...]
        count = experts * slots
        parts = part_in[moment].reshape(chips * slots, LANES)
        moe = dot(table, parts[0:count]) + dot(table, parts[count : 2 * count])
        kept = jnp.where(core * (1 - begun(moment)) == 1, x_all[0].astype(F32), x_res[moment].astype(F32))
        x_all[moment + 1] = (kept + moe).astype(BF16)
        return carry

    lax.fori_loop(0, sections, tick, 0)

    last = remote(x_all.at[sections], x_last, l_send.at[0], l_recv.at[0], device((0, 0), 1))
    last.start()
    lanes = lax.broadcasted_iota(jnp.int32, (rows, LANES), 1).astype(F32)

    def members(group_row):
        column = dot_t(eye[...], jnp.broadcast_to(group_row.astype(F32), (16, rows)).astype(BF16))[:, 0:1]
        return jnp.where(column == lanes, 1.0, 0.0)

    aim = jnp.where(core == 0, tgt[...].astype(F32), tgt_near[...].astype(F32))
    error = x_all[sections].astype(F32) - aim
    row_loss = jnp.sum(error * error, axis=1, keepdims=True) / width
    belongs = members(jnp.where(core == 0, gid[...], gid_near[...]))
    totals = jnp.sum(belongs * row_loss, axis=0, keepdims=True)
    counts = jnp.sum(belongs, axis=0, keepdims=True)
    red_rows = lax.broadcasted_iota(jnp.int32, (8, LANES), 0)
    local = jnp.where(red_rows == 0, totals, counts)
    red_mine[0] = local
    red_in[mine] = local

    def plane_copy(k, place):
        return remote(red_mine.at[0], red_in.at[place], s_send.at[k], s_recv.at[k], device(order[k]))

    for k in range(1, chips):
        plane_copy(k, mine).start()
    for k in range(1, chips):
        copy = plane_copy(k, place_of(order[k], -1))
        copy.wait_recv()
        copy.wait_send()
    plane = red_in[0]
    for j in range(1, chips):
        plane = plane + red_in[j]
    red_mine[1] = plane
    red_z[core, section] = plane
    steps = [(dz, swap) for dz in range(sections) for swap in range(2) if dz or swap]

    def depth_copy(n, lane_core, place):
        dz, swap = steps[n]
        return remote(
            red_mine.at[1], red_z.at[lane_core, place], sz_send.at[n], sz_recv.at[n], device((0, 0), dz, swap)
        )

    for n in range(len(steps)):
        depth_copy(n, core, section).start()
    for n, (dz, swap) in enumerate(steps):
        copy = depth_copy(n, other if swap else core, lax.rem(section + sections - dz, sections))
        copy.wait_recv()
        copy.wait_send()
    whole = red_z[0, 0]
    for n in range(1, 2 * sections):
        whole = whole + red_z[n // sections, n % sections]
    total = whole[0:1, :]
    count = whole[1:2, :] / (chips * 2)
    safe = jnp.maximum(count, 1.0)
    group_loss = total / safe
    lane_row = lax.broadcasted_iota(jnp.int32, (1, LANES), 1)
    raised = jnp.where(lane_row < GROUPS, jnp.exp(DRO_RATE * group_loss), 0.0)
    weight = raised / jnp.sum(raised, axis=1, keepdims=True) * (sections * rows) / safe
    row_weight = jnp.sum(members(gid[...]) * weight, axis=1, keepdims=True)
    last.wait_send()
    last.wait_recv()
    final = jnp.where(core == 0, x_all[sections].astype(F32), x_last[...].astype(F32))
    difference = final - tgt[...].astype(F32)
    grad_ref[...] = (row_weight * difference).astype(BF16)
    loss_ref[...] = group_loss[:, 0:GROUPS]


def per_device(
    slots, sent, groups, spread_out, tokens, targets, group_ids, expert_ids, norm_gain, router, w_gate, w_up, w_down
):
    sections = lax.axis_size("section")
    experts = lax.axis_size("expert")
    chips = experts * 2
    rows = tokens.shape[1]
    width = w_gate.shape[2]
    hidden = w_gate.shape[3]
    choices = jnp.transpose(expert_ids[0, 0], (0, 2, 1))
    router_rows = jnp.transpose(router[0])
    if experts < 8:
        router_rows = jnp.zeros((8, LANES), BF16).at[:experts].set(router_rows)
    vmem = pl.BlockSpec(memory_space=pltpu.VMEM)
    anywhere = pl.BlockSpec(memory_space=pl.ANY)
    dma = pltpu.SemaphoreType.DMA
    scratch = [
        pltpu.VMEM((2, chips, LANES, 2 * hidden), BF16),
        pltpu.VMEM((2, chips, hidden, LANES), BF16),
        pltpu.VMEM((sections + 1, rows, LANES), BF16),
        pltpu.VMEM((sections, rows, LANES), BF16),
        pltpu.VMEM((experts * slots, LANES), BF16),
        pltpu.VMEM((sections, 2, chips, slots, LANES), BF16),
        pltpu.VMEM((slots, 2 * hidden), F32),
        pltpu.VMEM((slots, LANES), F32),
        pltpu.VMEM((slots, 16), F32),
        pltpu.VMEM((2, slots, hidden), BF16),
        pltpu.VMEM((chips // spread_out, slots, spread_out * LANES), F32),
        pltpu.VMEM((chips, slots, LANES), BF16),
        pltpu.VMEM((sections, chips, slots, LANES), BF16),
        pltpu.VMEM((rows, LANES), BF16),
        pltpu.VMEM((1, rows), jnp.int32),
        pltpu.VMEM((sections, 2, rows), jnp.int32),
        pltpu.VMEM((1, LANES), F32),
        pltpu.VMEM((8, LANES), BF16),
        pltpu.VMEM((rows, LANES), BF16),
        pltpu.VMEM((1, rows), jnp.int32),
        pltpu.VMEM((sections, 2, rows), jnp.int32),
        pltpu.VMEM((1, LANES), F32),
        pltpu.VMEM((sections, 2, rows), jnp.int32),
        pltpu.VMEM((sections, 2, rows), jnp.int32),
        pltpu.VMEM((1, LANES), F32),
        pltpu.VMEM((rows, LANES), BF16),
        pltpu.VMEM((experts * slots, rows), BF16),
        pltpu.VMEM((rows, experts * slots), BF16),
        pltpu.VMEM((slots, 16), F32),
        pltpu.VMEM((rows, rows), BF16),
        pltpu.VMEM((rows, rows), BF16),
        pltpu.VMEM((16, LANES), F32),
        pltpu.VMEM((2, chips, 16, LANES), F32),
        pltpu.VMEM((2, 16, chips * LANES), BF16),
        pltpu.VMEM((2, 8, LANES), F32),
        pltpu.VMEM((chips, 8, LANES), F32),
        pltpu.VMEM((2, sections, 8, LANES), F32),
        dma((6,)),
        dma((4,)),
        dma((chips,)),
        dma((chips,)),
        dma((chips,)),
        dma((chips,)),
        dma((sections, chips)),
        dma((len(groups),)),
        dma((len(groups),)),
        dma((1,)),
        dma((1,)),
        dma((chips,)),
        dma((sections,)),
        dma((sections,)),
        dma((1,)),
        dma((sections,)),
        dma((chips,)),
        dma((chips,)),
        dma((1,)),
        dma((1,)),
        dma((4,)),
        dma((4,)),
        dma((chips,)),
        dma((chips,)),
        dma((2 * sections - 1,)),
        dma((2 * sections - 1,)),
        dma((1,)),
        dma((1,)),
    ]
    grad, loss = pl.pallas_call(
        functools.partial(kernel, sections, experts, slots, sent, groups, spread_out, float(width)),
        out_shape=(
            jax.ShapeDtypeStruct((rows, LANES), BF16),
            jax.ShapeDtypeStruct((1, GROUPS), F32),
        ),
        in_specs=[anywhere] * 9,
        out_specs=(vmem, vmem),
        scratch_shapes=scratch,
        compiler_params=pltpu.CompilerParams(
            collective_id=0, has_side_effects=True, vmem_limit_bytes=60 * 1024 * 1024
        ),
        name="moe_ring",
    )(
        tokens[0],
        targets[0],
        group_ids,
        choices,
        norm_gain,
        router_rows,
        w_gate.reshape(chips, 2, LANES, hidden),
        w_up.reshape(chips, 2, LANES, hidden),
        w_down.reshape(hidden, width),
    )
    return grad[None], loss[0]


def build(mesh, slots, sent, groups, spread_out):
    placed = (
        P("section", None, ("expert", "dp")),
        P("section", None, ("expert", "dp")),
        P("section", None),
        P(None, "section", None, None, None),
        P("section", ("expert", "dp")),
        P("section", ("expert", "dp"), None),
        P("section", "expert", None, "dp"),
        P("section", "expert", None, "dp"),
        P("section", "expert", "dp", None),
    )
    return jax.shard_map(
        functools.partial(per_device, slots, sent, groups, spread_out),
        mesh=mesh,
        in_specs=placed,
        out_specs=(P("section", None, ("expert", "dp")), P()),
        check_vma=False,
    )


def solution(mesh):
    return build(mesh, 80, 72, ((0, 8), (8, 16)), 4)
```

```python
import functools

import jax
import jax.numpy as jnp
from jax import lax
from jax.experimental import pallas as pl
from jax.experimental.pallas import tpu as pltpu
from jax.sharding import PartitionSpec as P

MESH = pl.DeviceIdType.MESH
GROUPS = 8
TOPK = 2
DRO_RATE = 0.3
LANES = 128
F32 = jnp.float32
BF16 = jnp.bfloat16
LAST_DIMS = (((1,), (1,)), ((), ()))


def dot(a, b):
    return jnp.dot(a, b, preferred_element_type=F32)


def dot_t(a, b):
    return lax.dot_general(a, b, LAST_DIMS, preferred_element_type=F32)


def ones_where(mask):
    return jnp.where(mask, 1.0, 0.0).astype(BF16)


def kernel(
    sections, experts, slots, sent, groups, spread_out, width,
    tok_ref, tgt_ref, gid_ref, ids_ref, gain_ref, rt_ref, wg_ref, wu_ref, wd_ref,
    grad_ref, loss_ref,
    w_gu, w_dn, x_all, x_res, out_buf, x_in, acc, sq_acc, logit_acc, act, dn_acc, part_out, part_in,
    tgt, gid, ids, gain_row, rt_raw, tgt_near, gid_near, ids_near, gain_near, ids_out, ids_back, gain_out, x_last,
    pick, scat, chosen_mask, upper, eye, rt_mine, rt_in, rt_bf, red_mine, red_in, red_z,
    in_sem, w_sem, wd_sem, wd_send, wd_recv, d_send, d_recv, f_send, f_recv, a_send, a_recv,
    c_send, c_recv, c_own, z_send, z_recv, r_send, r_recv, rf_send, rf_recv, n_send, n_recv, s_send, s_recv,
    sz_send, sz_recv, l_send, l_recv,
):
    chips = experts * 2
    across = 4
    down = chips // across
    rows = tok_ref.shape[0]
    hidden = wg_ref.shape[-1]
    section = lax.axis_index("section")
    expert = lax.axis_index("expert")
    lane = lax.axis_index("dp")
    core = lax.rem(lane, 2)
    half = lane // 2
    x_place = lax.rem(expert, across)
    y_place = expert // across * 2 + half
    mine = expert * 2 + half
    other = 1 - core
    sibling = (section, expert, half * 2 + other)

    def hops(offset):
        return min(offset[0], across - offset[0]) + min(offset[1], down - offset[1])

    offsets = [(dx, dy) for dx in range(across) for dy in range(down)]
    order = [(0, 0)] + sorted(offsets[1:], key=lambda offset: -hops(offset))
    sends = order[1:] + order[:1]

    def chip(offset, sign=1):
        x = lax.rem(x_place + across + sign * offset[0], across)
        y = lax.rem(y_place + down + sign * offset[1], down)
        return y // 2 * across + x, lax.rem(y, 2)

    def place_of(offset, sign=1):
        e, h = chip(offset, sign)
        return e * 2 + h

    def device(offset, on=0, swap=0):
        e, h = chip(offset)
        return (lax.rem(section + on, sections), e, h * 2 + (other if swap else core))

    def remote(src, dst, send, recv, target):
        return pltpu.make_async_remote_copy(
            src_ref=src, dst_ref=dst, send_sem=send, recv_sem=recv, device_id=target, device_id_type=MESH
        )

    inputs = [
        pltpu.make_async_copy(src, dst, in_sem.at[n])
        for n, (src, dst) in enumerate(
            [(ids_ref, ids), (tok_ref, x_all.at[0]), (gain_ref, gain_row), (rt_ref, rt_raw), (tgt_ref, tgt), (gid_ref, gid)]
        )
    ]
    loads = []
    for side in range(2):
        loads.append(pltpu.make_async_copy(wg_ref.at[:, side], w_gu.at[side, :, :, 0:hidden], w_sem.at[2 * side]))
        loads.append(
            pltpu.make_async_copy(wu_ref.at[:, side], w_gu.at[side, :, :, hidden : 2 * hidden], w_sem.at[2 * side + 1])
        )
    for j in range(chips):
        own_columns = pl.ds(pl.multiple_of(j * 2 * LANES + core * LANES, LANES), LANES)
        loads.append(pltpu.make_async_copy(wd_ref.at[:, own_columns], w_dn.at[core, j], wd_sem.at[j]))
    for load in inputs:
        load.start()

    part_in[:, :, sent:slots, :] = jnp.zeros((sections, chips, slots - sent, LANES), BF16)

    barrier = pltpu.get_barrier_semaphore()
    partners = {(dx, dy, 0, 0) for dx, dy in offsets[1:]} | {(0, 0, 0, 1)}
    partners |= {(dx, dy, dz % sections, 0) for dx, dy in offsets for dz in (1, -1)}
    partners |= {(0, 0, dz, swap) for dz in range(1, sections) for swap in range(2)}
    for dx, dy, dz, swap in sorted(partners):
        pl.semaphore_signal(barrier, inc=1, device_id=device((dx, dy), dz, swap), device_id_type=MESH)
    for load in loads:
        load.start()

    first = lax.broadcasted_iota(jnp.int32, (rows, rows), 0)
    second = lax.broadcasted_iota(jnp.int32, (rows, rows), 1)
    upper[...] = ones_where(first < second)
    eye[...] = ones_where(first == second)
    for load in inputs:
        load.wait()
    gain = gain_row[...]
    rt_mine[0:8, :] = rt_raw[...].astype(F32)
    rt_mine[8:16, :] = jnp.broadcast_to(1.0 / (gain * gain), (8, LANES))
    rt_in[core, 0] = rt_mine[...]
    gain_out[...] = gain

    expert_rows = lax.broadcasted_iota(jnp.int32, (16, rows), 0)

    slot_rows = lax.broadcasted_iota(jnp.int32, (slots, rows), 0).astype(F32)

    def micro_of(place):
        return lax.rem(place + 2 * sections, sections)

    def ranks(table, micro):
        first_id = table[micro, 0:1, :]
        second_id = table[micro, 1:2, :]
        hit_first = first_id == expert_rows
        hit_second = second_id == expert_rows
        either = hit_first | hit_second
        named = ones_where(either)
        return first_id, second_id, hit_first, hit_second, either, named, dot(named, upper[...])

    def prepare_pick(table, micro):
        _, _, _, _, either, _, rank = ranks(table, micro)
        key = jnp.where(either, rank, -1.0)
        for e in range(experts):
            pick[e * slots : (e + 1) * slots, :] = ones_where(key[e : e + 1, :] == slot_rows)

    def prepare_mask(moment):
        _, _, _, _, either, named, rank = ranks(ids, micro_of(section - moment))
        key = jnp.sum(jnp.where(expert_rows == expert, jnp.where(either, rank, -1.0), 0.0), axis=0, keepdims=True)
        chosen_mask[...] = dot_t(ones_where(key == slot_rows), named)

    def prepare_scatter(moment):
        first_id, second_id, hit_first, hit_second, _, _, rank = ranks(
            ids_back, micro_of(section + core - 1 - moment)
        )
        rank_first = jnp.sum(jnp.where(hit_first, rank, 0.0), axis=0, keepdims=True)
        rank_second = jnp.sum(jnp.where(hit_second, rank, 0.0), axis=0, keepdims=True)
        table = jnp.where(expert_rows == 0, first_id.astype(F32), second_id.astype(F32))
        table = jnp.where(expert_rows == 2, rank_first, table)
        table = jnp.where(expert_rows == 3, rank_second, table)
        spread = dot_t(eye[...], table.astype(BF16))
        slot_first = spread[:, 0:1] * slots + spread[:, 2:3]
        slot_second = spread[:, 1:2] * slots + spread[:, 3:4]
        lanes = lax.broadcasted_iota(jnp.int32, (rows, LANES), 1).astype(F32)
        for n in range(experts * slots // LANES):
            here = lanes + float(n * LANES)
            scat[:, n * LANES : (n + 1) * LANES] = ones_where((slot_first == here) | (slot_second == here))

    prepare_pick(ids, section)

    pl.semaphore_wait(barrier, len(partners))

    def router_copy(k):
        return remote(rt_mine, rt_in.at[core, k], r_send.at[k], r_recv.at[k], device(order[k]))

    toward = device((0, 0), sections + 1 - 2 * core)
    neighbour = [
        remote(src, dst, n_send.at[n], n_recv.at[n], toward)
        for n, (src, dst) in enumerate([(ids, ids_near), (gain_row, gain_near), (gid, gid_near), (tgt, tgt_near)])
    ]

    def down_copy(j):
        sib_columns = pl.ds(pl.multiple_of(j * 2 * LANES + other * LANES, LANES), LANES)
        return remote(wd_ref.at[:, sib_columns], w_dn.at[core, j], wd_send.at[j], wd_recv.at[j], sibling)

    for k in range(1, chips):
        router_copy(k).start()
    for copy in neighbour:
        copy.start()

    def begun(moment):
        return 1 - (sections - moment) // sections

    def stays(moment):
        return core * begun(moment) == 0

    def dispatch_copy(k, moment):
        e, _ = chip(order[k])
        block = pl.ds(pl.multiple_of(e * slots, 16), sent)
        return remote(
            out_buf.at[block, :], x_in.at[moment, core, k, pl.ds(0, sent)], d_send.at[k], d_recv.at[moment, k],
            device(order[k], core * begun(moment)),
        )

    def dispatch(moment):
        scaled = (x_all[moment].astype(F32) * gain_out[...]).astype(BF16)
        out_buf[...] = dot(pick[...], scaled).astype(BF16)
        for k in range(1, chips):
            dispatch_copy(k, moment).start()

        @pl.when(stays(moment))
        def _():
            x_in[moment, core, 0] = out_buf[pl.ds(pl.multiple_of(expert * slots, 16), slots), :]

        @pl.when(jnp.logical_not(stays(moment)))
        def _():
            dispatch_copy(0, moment).start()

    def router_forward(source):
        return remote(rt_in.at[source], rt_in.at[source], rf_send.at[0], rf_recv.at[0], sibling)

    def round_router(source):
        for k in range(chips):
            rt_bf[source, :, k * LANES : (k + 1) * LANES] = rt_in[source, k].astype(BF16)

    def first_tick():
        for j in range(chips):
            down_copy(j).start()
        for k in range(1, chips):
            copy = router_copy(k)
            copy.wait_recv()
            copy.wait_send()
        router_forward(core).start()
        for copy in neighbour:
            copy.wait_recv()
            copy.wait_send()
        ids_out[...] = jnp.where(core == 0, ids[...], ids_near[...])
        ids_back[...] = jnp.where(core == 0, ids_near[...], ids[...])
        gain_out[...] = jnp.where(core == 0, gain_row[...], gain_near[...])
        round_router(core)
        for load in loads:
            load.wait()

    def router_here():
        router_forward(core).wait_send()
        router_forward(other).wait_recv()
        round_router(other)

    def down_here():
        for j in range(chips):
            copy = remote(wd_ref.at[:, pl.ds(0, LANES)], w_dn.at[other, j], wd_send.at[j], wd_recv.at[j], sibling)
            copy.wait_send()
            copy.wait_recv()

    group_count = len(groups)

    def group_work(moment, source, g, fresh):
        start, stop = groups[g]
        ks = range(start, stop)
        blocks = [x_in[moment, source, k] for k in ks]
        block = jnp.concatenate(blocks, axis=1)
        weight = jnp.concatenate([w_gu[source, place_of(order[k], -1)] for k in ks], axis=0)
        product = dot(block, weight)
        router = rt_bf[source, :, start * LANES : stop * LANES]
        logits = dot_t(block, router)
        squares = None
        for k, piece in zip(ks, blocks):
            wide = piece.astype(F32)
            term = wide * wide * rt_in[source, k, 8:9, :]
            squares = term if squares is None else squares + term
        if fresh:
            acc[...] = product
            logit_acc[...] = logits
            sq_acc[...] = squares
        else:
            acc[...] += product
            logit_acc[...] += logits
            sq_acc[...] += squares

    def forward_copy(source, g, moment):
        block = x_in.at[moment, source, pl.ds(groups[g][0], groups[g][1] - groups[g][0])]
        return remote(block, block, f_send.at[g], f_recv.at[g], sibling)

    def own_group(g, moment, fresh=False):
        if g == 0:

            @pl.when(jnp.logical_not(stays(moment)))
            def _():
                dispatch_copy(0, moment).wait_recv()

        for k in range(max(1, groups[g][0]), groups[g][1]):
            dispatch_copy(k, moment).wait_recv()
        forward_copy(core, g, moment).start()
        group_work(moment, core, g, fresh)

    def sibling_group(g, moment):
        forward_copy(other, g, moment).wait_recv()
        group_work(moment, other, g, False)

    pairs = [tuple(range(n, n + spread_out)) for n in range(0, chips, spread_out)]

    def tick(moment, carry):
        dispatch(moment)
        ahead = remote(
            x_all.at[moment], x_res.at[moment], z_send.at[0], z_recv.at[moment], device((0, 0), 1)
        )
        ahead.start()

        @pl.when(moment == 0)
        def _():
            first_tick()

        prepare_mask(moment)
        prepare_scatter(moment)

        own_group(0, moment, True)
        for g in range(1, group_count):
            own_group(g, moment)
            if g == 1:
                pl.when(moment == 0)(router_here)
            sibling_group(g - 1, moment)
        sibling_group(group_count - 1, moment)

        row_scale = lax.rsqrt(jnp.sum(sq_acc[...], axis=1, keepdims=True) / width + 1e-6)
        gate_part = acc[:, 0:hidden] * row_scale
        up_part = acc[:, hidden : 2 * hidden] * row_scale
        act[core] = (gate_part / (1.0 + jnp.exp(-gate_part)) * up_part).astype(BF16)
        swap = remote(act.at[core], act.at[core], a_send.at[0], a_recv.at[0], sibling)
        swap.start()

        chosen = chosen_mask[...] > 0.5
        logits = logit_acc[...] * row_scale
        lanes = lax.broadcasted_iota(jnp.int32, (slots, 16), 1)
        top = jnp.max(jnp.where(chosen, logits, -1e30), axis=1, keepdims=True)
        raised = jnp.where(chosen, jnp.exp(jnp.where(chosen, logits - top, 0.0)), 0.0)
        gate = jnp.sum(jnp.where(lanes == expert, raised, 0.0), axis=1, keepdims=True) / jnp.maximum(
            jnp.sum(raised, axis=1, keepdims=True), 1e-30
        )

        def down_weight(source, pair):
            return jnp.concatenate([w_dn[source, place_of(sends[n])] for n in pair], axis=1)

        own_act = act[core]
        for i, pair in enumerate(pairs):
            dn_acc[i] = dot(own_act, down_weight(core, pair))
        @pl.when(moment == 0)
        def _():
            down_here()

        remote(act.at[other], act.at[other], a_send.at[0], a_recv.at[0], sibling).wait_recv()
        sib_act = act[other]
        landing = half * experts + expert

        def part_copy(n):
            return remote(
                part_out.at[n, pl.ds(0, sent)], part_in.at[moment, landing, pl.ds(0, sent)], c_send.at[n],
                c_own.at[moment] if n == chips - 1 else c_recv.at[moment], device(sends[n], 1 - core),
            )

        for i, pair in enumerate(pairs):
            piece = ((dn_acc[i] + dot(sib_act, down_weight(other, pair))) * gate).astype(BF16)
            for at, n in enumerate(pair):
                value = piece[:, at * LANES : (at + 1) * LANES]
                part_out[n] = value
                if n < chips - 1:
                    part_copy(n).start()
                else:

                    @pl.when(core == 0)
                    def _(n=n):
                        part_copy(n).start()

                    @pl.when(core == 1)
                    def _(value=value):
                        part_in[moment, landing, 0:sent, :] = value[0:sent, :]

        prepare_pick(ids_out, micro_of(section + core - moment - 1))

        swap.wait_send()
        for g in range(group_count):
            forward_copy(core, g, moment).wait_send()
        for k in range(1, chips):
            dispatch_copy(k, moment).wait_send()

        @pl.when(jnp.logical_not(stays(moment)))
        def _():
            dispatch_copy(0, moment).wait_send()

        for n in range(chips - 1):
            part_copy(n).wait_send()

        @pl.when(core == 0)
        def _():
            part_copy(chips - 1).wait_send()
            part_copy(chips - 1).wait_recv()

        ahead.wait_send()
        ahead.wait_recv()
        everything = part_in.at[moment, pl.ds(0, chips - 1), pl.ds(0, sent)]
        remote(everything, everything, c_send.at[0], c_recv.at[moment], device((0, 0), 1)).wait_recv()
        table = scat[...]
        count = experts * slots
        parts = part_in[moment].reshape(chips * slots, LANES)
        moe = dot(table, parts[0:count]) + dot(table, parts[count : 2 * count])
        kept = jnp.where(core * (1 - begun(moment)) == 1, x_all[0].astype(F32), x_res[moment].astype(F32))
        x_all[moment + 1] = (kept + moe).astype(BF16)
        return carry

    lax.fori_loop(0, sections, tick, 0)

    last = remote(x_all.at[sections], x_last, l_send.at[0], l_recv.at[0], device((0, 0), 1))
    last.start()
    lanes = lax.broadcasted_iota(jnp.int32, (rows, LANES), 1).astype(F32)

    def members(group_row):
        column = dot_t(eye[...], jnp.broadcast_to(group_row.astype(F32), (16, rows)).astype(BF16))[:, 0:1]
        return jnp.where(column == lanes, 1.0, 0.0)

    aim = jnp.where(core == 0, tgt[...].astype(F32), tgt_near[...].astype(F32))
    error = x_all[sections].astype(F32) - aim
    row_loss = jnp.sum(error * error, axis=1, keepdims=True) / width
    belongs = members(jnp.where(core == 0, gid[...], gid_near[...]))
    totals = jnp.sum(belongs * row_loss, axis=0, keepdims=True)
    counts = jnp.sum(belongs, axis=0, keepdims=True)
    red_rows = lax.broadcasted_iota(jnp.int32, (8, LANES), 0)
    local = jnp.where(red_rows == 0, totals, counts)
    red_mine[0] = local
    red_in[mine] = local

    def plane_copy(k, place):
        return remote(red_mine.at[0], red_in.at[place], s_send.at[k], s_recv.at[k], device(order[k]))

    for k in range(1, chips):
        plane_copy(k, mine).start()
    own_members = members(gid[...])
    for k in range(1, chips):
        copy = plane_copy(k, place_of(order[k], -1))
        copy.wait_recv()
        copy.wait_send()
    plane = red_in[0]
    for j in range(1, chips):
        plane = plane + red_in[j]
    red_mine[1] = plane
    red_z[core, section] = plane
    steps = [(dz, swap) for dz in range(sections) for swap in range(2) if dz or swap]

    def depth_copy(n, lane_core, place):
        dz, swap = steps[n]
        return remote(
            red_mine.at[1], red_z.at[lane_core, place], sz_send.at[n], sz_recv.at[n], device((0, 0), dz, swap)
        )

    for n in range(len(steps)):
        depth_copy(n, core, section).start()
    for n, (dz, swap) in enumerate(steps):
        copy = depth_copy(n, other if swap else core, lax.rem(section + sections - dz, sections))
        copy.wait_recv()
        copy.wait_send()
    whole = red_z[0, 0]
    for n in range(1, 2 * sections):
        whole = whole + red_z[n // sections, n % sections]
    total = whole[0:1, :]
    count = whole[1:2, :] / (chips * 2)
    safe = jnp.maximum(count, 1.0)
    group_loss = total / safe
    lane_row = lax.broadcasted_iota(jnp.int32, (1, LANES), 1)
    raised = jnp.where(lane_row < GROUPS, jnp.exp(DRO_RATE * group_loss), 0.0)
    weight = raised / jnp.sum(raised, axis=1, keepdims=True) * (sections * rows) / safe
    row_weight = jnp.sum(own_members * weight, axis=1, keepdims=True)
    last.wait_send()
    last.wait_recv()
    final = jnp.where(core == 0, x_all[sections].astype(F32), x_last[...].astype(F32))
    difference = final - tgt[...].astype(F32)
    grad_ref[...] = (row_weight * difference).astype(BF16)
    loss_ref[...] = group_loss[:, 0:GROUPS]


def per_device(
    slots, sent, groups, spread_out, tokens, targets, group_ids, expert_ids, norm_gain, router, w_gate, w_up, w_down
):
    sections = lax.axis_size("section")
    experts = lax.axis_size("expert")
    chips = experts * 2
    rows = tokens.shape[1]
    width = w_gate.shape[2]
    hidden = w_gate.shape[3]
    choices = jnp.transpose(expert_ids[0, 0], (0, 2, 1))
    router_rows = jnp.transpose(router[0])
    if experts < 8:
        router_rows = jnp.zeros((8, LANES), BF16).at[:experts].set(router_rows)
    vmem = pl.BlockSpec(memory_space=pltpu.VMEM)
    anywhere = pl.BlockSpec(memory_space=pl.ANY)
    dma = pltpu.SemaphoreType.DMA
    scratch = [
        pltpu.VMEM((2, chips, LANES, 2 * hidden), BF16),
        pltpu.VMEM((2, chips, hidden, LANES), BF16),
        pltpu.VMEM((sections + 1, rows, LANES), BF16),
        pltpu.VMEM((sections, rows, LANES), BF16),
        pltpu.VMEM((experts * slots, LANES), BF16),
        pltpu.VMEM((sections, 2, chips, slots, LANES), BF16),
        pltpu.VMEM((slots, 2 * hidden), F32),
        pltpu.VMEM((slots, LANES), F32),
        pltpu.VMEM((slots, 16), F32),
        pltpu.VMEM((2, slots, hidden), BF16),
        pltpu.VMEM((chips // spread_out, slots, spread_out * LANES), F32),
        pltpu.VMEM((chips, slots, LANES), BF16),
        pltpu.VMEM((sections, chips, slots, LANES), BF16),
        pltpu.VMEM((rows, LANES), BF16),
        pltpu.VMEM((1, rows), jnp.int32),
        pltpu.VMEM((sections, 2, rows), jnp.int32),
        pltpu.VMEM((1, LANES), F32),
        pltpu.VMEM((8, LANES), BF16),
        pltpu.VMEM((rows, LANES), BF16),
        pltpu.VMEM((1, rows), jnp.int32),
        pltpu.VMEM((sections, 2, rows), jnp.int32),
        pltpu.VMEM((1, LANES), F32),
        pltpu.VMEM((sections, 2, rows), jnp.int32),
        pltpu.VMEM((sections, 2, rows), jnp.int32),
        pltpu.VMEM((1, LANES), F32),
        pltpu.VMEM((rows, LANES), BF16),
        pltpu.VMEM((experts * slots, rows), BF16),
        pltpu.VMEM((rows, experts * slots), BF16),
        pltpu.VMEM((slots, 16), F32),
        pltpu.VMEM((rows, rows), BF16),
        pltpu.VMEM((rows, rows), BF16),
        pltpu.VMEM((16, LANES), F32),
        pltpu.VMEM((2, chips, 16, LANES), F32),
        pltpu.VMEM((2, 16, chips * LANES), BF16),
        pltpu.VMEM((2, 8, LANES), F32),
        pltpu.VMEM((chips, 8, LANES), F32),
        pltpu.VMEM((2, sections, 8, LANES), F32),
        dma((6,)),
        dma((4,)),
        dma((chips,)),
        dma((chips,)),
        dma((chips,)),
        dma((chips,)),
        dma((sections, chips)),
        dma((len(groups),)),
        dma((len(groups),)),
        dma((1,)),
        dma((1,)),
        dma((chips,)),
        dma((sections,)),
        dma((sections,)),
        dma((1,)),
        dma((sections,)),
        dma((chips,)),
        dma((chips,)),
        dma((1,)),
        dma((1,)),
        dma((4,)),
        dma((4,)),
        dma((chips,)),
        dma((chips,)),
        dma((2 * sections - 1,)),
        dma((2 * sections - 1,)),
        dma((1,)),
        dma((1,)),
    ]
    grad, loss = pl.pallas_call(
        functools.partial(kernel, sections, experts, slots, sent, groups, spread_out, float(width)),
        out_shape=(
            jax.ShapeDtypeStruct((rows, LANES), BF16),
            jax.ShapeDtypeStruct((1, GROUPS), F32),
        ),
        in_specs=[anywhere] * 9,
        out_specs=(vmem, vmem),
        scratch_shapes=scratch,
        compiler_params=pltpu.CompilerParams(
            collective_id=0, has_side_effects=True, vmem_limit_bytes=60 * 1024 * 1024
        ),
        name="moe_ring",
    )(
        tokens[0],
        targets[0],
        group_ids,
        choices,
        norm_gain,
        router_rows,
        w_gate.reshape(chips, 2, LANES, hidden),
        w_up.reshape(chips, 2, LANES, hidden),
        w_down.reshape(hidden, width),
    )
    return grad[None], loss[0]


def build(mesh, slots, sent, groups, spread_out):
    placed = (
        P("section", None, ("expert", "dp")),
        P("section", None, ("expert", "dp")),
        P("section", None),
        P(None, "section", None, None, None),
        P("section", ("expert", "dp")),
        P("section", ("expert", "dp"), None),
        P("section", "expert", None, "dp"),
        P("section", "expert", None, "dp"),
        P("section", "expert", "dp", None),
    )
    return jax.shard_map(
        functools.partial(per_device, slots, sent, groups, spread_out),
        mesh=mesh,
        in_specs=placed,
        out_specs=(P("section", None, ("expert", "dp")), P()),
        check_vma=False,
    )


def solution(mesh):
    return build(mesh, 80, 72, ((0, 8), (8, 16)), 4)
```

```python
import functools

import jax
import jax.numpy as jnp
from jax import lax
from jax.experimental import pallas as pl
from jax.experimental.pallas import tpu as pltpu
from jax.sharding import PartitionSpec as P

MESH = pl.DeviceIdType.MESH
GROUPS = 8
TOPK = 2
DRO_RATE = 0.3
LANES = 128
F32 = jnp.float32
BF16 = jnp.bfloat16
LAST_DIMS = (((1,), (1,)), ((), ()))


def dot(a, b):
    return jnp.dot(a, b, preferred_element_type=F32)


def dot_t(a, b):
    return lax.dot_general(a, b, LAST_DIMS, preferred_element_type=F32)


def ones_where(mask):
    return jnp.where(mask, 1.0, 0.0).astype(BF16)


def kernel(
    sections, experts, slots, sent, groups, spread_out, width,
    tok_ref, tgt_ref, gid_ref, ids_ref, gain_ref, rt_ref, wg_ref, wu_ref, wd_ref,
    grad_ref, loss_ref,
    w_gu, w_dn, x_all, x_res, out_buf, x_in, acc, sq_acc, logit_acc, act, dn_acc, part_out, part_in,
    tgt, gid, ids, gain_row, rt_raw, tgt_near, gid_near, ids_near, gain_near, ids_out, ids_back, gain_out, x_last,
    pick, scat, chosen_mask, upper, eye, rt_mine, rt_in, rt_bf, red_mine, red_in, red_z,
    in_sem, w_sem, wd_sem, wd_send, wd_recv, d_send, d_recv, f_send, f_recv, a_send, a_recv,
    c_send, c_recv, c_own, z_send, z_recv, r_send, r_recv, rf_send, rf_recv, n_send, n_recv, s_send, s_recv,
    sz_send, sz_recv, l_send, l_recv,
):
    chips = experts * 2
    across = 4
    down = chips // across
    rows = tok_ref.shape[0]
    hidden = wg_ref.shape[-1]
    section = lax.axis_index("section")
    expert = lax.axis_index("expert")
    lane = lax.axis_index("dp")
    core = lax.rem(lane, 2)
    half = lane // 2
    x_place = lax.rem(expert, across)
    y_place = expert // across * 2 + half
    mine = expert * 2 + half
    other = 1 - core
    sibling = (section, expert, half * 2 + other)

    def hops(offset):
        return min(offset[0], across - offset[0]) + min(offset[1], down - offset[1])

    offsets = [(dx, dy) for dx in range(across) for dy in range(down)]
    order = [(0, 0)] + sorted(offsets[1:], key=lambda offset: -hops(offset))
    sends = order[1:] + order[:1]

    def chip(offset, sign=1):
        x = lax.rem(x_place + across + sign * offset[0], across)
        y = lax.rem(y_place + down + sign * offset[1], down)
        return y // 2 * across + x, lax.rem(y, 2)

    def place_of(offset, sign=1):
        e, h = chip(offset, sign)
        return e * 2 + h

    def device(offset, on=0, swap=0):
        e, h = chip(offset)
        return (lax.rem(section + on, sections), e, h * 2 + (other if swap else core))

    def remote(src, dst, send, recv, target):
        return pltpu.make_async_remote_copy(
            src_ref=src, dst_ref=dst, send_sem=send, recv_sem=recv, device_id=target, device_id_type=MESH
        )

    inputs = [
        pltpu.make_async_copy(src, dst, in_sem.at[n])
        for n, (src, dst) in enumerate(
            [(ids_ref, ids), (tok_ref, x_all.at[0]), (gain_ref, gain_row), (rt_ref, rt_raw), (tgt_ref, tgt), (gid_ref, gid)]
        )
    ]
    loads = []
    for side in range(2):
        loads.append(pltpu.make_async_copy(wg_ref.at[:, side], w_gu.at[side, :, :, 0:hidden], w_sem.at[2 * side]))
        loads.append(
            pltpu.make_async_copy(wu_ref.at[:, side], w_gu.at[side, :, :, hidden : 2 * hidden], w_sem.at[2 * side + 1])
        )
    for j in range(chips):
        own_columns = pl.ds(pl.multiple_of(j * 2 * LANES + core * LANES, LANES), LANES)
        loads.append(pltpu.make_async_copy(wd_ref.at[:, own_columns], w_dn.at[core, j], wd_sem.at[j]))
    for load in inputs:
        load.start()

    part_in[:, :, sent:slots, :] = jnp.zeros((sections, chips, slots - sent, LANES), BF16)

    barrier = pltpu.get_barrier_semaphore()
    partners = {(dx, dy, 0, 0) for dx, dy in offsets[1:]} | {(0, 0, 0, 1)}
    partners |= {(dx, dy, dz % sections, 0) for dx, dy in offsets for dz in (1, -1)}
    partners |= {(0, 0, dz, swap) for dz in range(1, sections) for swap in range(2)}
    for dx, dy, dz, swap in sorted(partners):
        pl.semaphore_signal(barrier, inc=1, device_id=device((dx, dy), dz, swap), device_id_type=MESH)
    for load in loads:
        load.start()

    first = lax.broadcasted_iota(jnp.int32, (rows, rows), 0)
    second = lax.broadcasted_iota(jnp.int32, (rows, rows), 1)
    upper[...] = ones_where(first < second)
    eye[...] = ones_where(first == second)
    for load in inputs:
        load.wait()
    gain = gain_row[...]
    rt_mine[0:8, :] = rt_raw[...].astype(F32)
    rt_mine[8:16, :] = jnp.broadcast_to(1.0 / (gain * gain), (8, LANES))
    rt_in[core, 0] = rt_mine[...]
    gain_out[...] = gain

    expert_rows = lax.broadcasted_iota(jnp.int32, (16, rows), 0)

    slot_rows = lax.broadcasted_iota(jnp.int32, (slots, rows), 0).astype(F32)

    def micro_of(place):
        return lax.rem(place + 2 * sections, sections)

    def ranks(table, micro):
        first_id = table[micro, 0:1, :]
        second_id = table[micro, 1:2, :]
        hit_first = first_id == expert_rows
        hit_second = second_id == expert_rows
        either = hit_first | hit_second
        named = ones_where(either)
        return first_id, second_id, hit_first, hit_second, either, named, dot(named, upper[...])

    def prepare_pick(table, micro):
        _, _, _, _, either, _, rank = ranks(table, micro)
        key = jnp.where(either, rank, -1.0)
        for e in range(experts):
            pick[e * slots : (e + 1) * slots, :] = ones_where(key[e : e + 1, :] == slot_rows)

    def prepare_mask(moment):
        _, _, _, _, either, named, rank = ranks(ids, micro_of(section - moment))
        key = jnp.sum(jnp.where(expert_rows == expert, jnp.where(either, rank, -1.0), 0.0), axis=0, keepdims=True)
        chosen_mask[...] = dot_t(ones_where(key == slot_rows), named)

    def prepare_scatter(moment):
        first_id, second_id, hit_first, hit_second, _, _, rank = ranks(
            ids_back, micro_of(section + core - 1 - moment)
        )
        rank_first = jnp.sum(jnp.where(hit_first, rank, 0.0), axis=0, keepdims=True)
        rank_second = jnp.sum(jnp.where(hit_second, rank, 0.0), axis=0, keepdims=True)
        table = jnp.where(expert_rows == 0, first_id.astype(F32), second_id.astype(F32))
        table = jnp.where(expert_rows == 2, rank_first, table)
        table = jnp.where(expert_rows == 3, rank_second, table)
        spread = dot_t(eye[...], table.astype(BF16))
        slot_first = spread[:, 0:1] * slots + spread[:, 2:3]
        slot_second = spread[:, 1:2] * slots + spread[:, 3:4]
        lanes = lax.broadcasted_iota(jnp.int32, (rows, LANES), 1).astype(F32)
        for n in range(experts * slots // LANES):
            here = lanes + float(n * LANES)
            scat[:, n * LANES : (n + 1) * LANES] = ones_where((slot_first == here) | (slot_second == here))

    prepare_pick(ids, section)

    pl.semaphore_wait(barrier, len(partners))

    def router_copy(k):
        return remote(rt_mine, rt_in.at[core, k], r_send.at[k], r_recv.at[k], device(order[k]))

    toward = device((0, 0), sections + 1 - 2 * core)
    neighbour = [
        remote(src, dst, n_send.at[n], n_recv.at[n], toward)
        for n, (src, dst) in enumerate([(ids, ids_near), (gain_row, gain_near), (gid, gid_near), (tgt, tgt_near)])
    ]

    def down_copy(j):
        sib_columns = pl.ds(pl.multiple_of(j * 2 * LANES + other * LANES, LANES), LANES)
        return remote(wd_ref.at[:, sib_columns], w_dn.at[core, j], wd_send.at[j], wd_recv.at[j], sibling)

    for k in range(1, chips):
        router_copy(k).start()
    for copy in neighbour:
        copy.start()

    def begun(moment):
        return 1 - (sections - moment) // sections

    def stays(moment):
        return core * begun(moment) == 0

    def dispatch_copy(k, moment):
        e, _ = chip(order[k])
        block = pl.ds(pl.multiple_of(e * slots, 16), sent)
        return remote(
            out_buf.at[block, :], x_in.at[moment, core, k, pl.ds(0, sent)], d_send.at[k], d_recv.at[moment, k],
            device(order[k], core * begun(moment)),
        )

    def dispatch(moment):
        scaled = (x_all[moment].astype(F32) * gain_out[...]).astype(BF16)
        out_buf[...] = dot(pick[...], scaled).astype(BF16)
        @pl.when(jnp.logical_not(stays(moment)))
        def _():
            dispatch_copy(0, moment).start()

        for k in range(1, chips):
            dispatch_copy(k, moment).start()

        @pl.when(stays(moment))
        def _():
            x_in[moment, core, 0] = out_buf[pl.ds(pl.multiple_of(expert * slots, 16), slots), :]

    def router_forward(source):
        return remote(rt_in.at[source], rt_in.at[source], rf_send.at[0], rf_recv.at[0], sibling)

    def round_router(source):
        for k in range(chips):
            rt_bf[source, :, k * LANES : (k + 1) * LANES] = rt_in[source, k].astype(BF16)

    def first_tick():
        for j in range(chips):
            down_copy(j).start()
        for k in range(1, chips):
            copy = router_copy(k)
            copy.wait_recv()
            copy.wait_send()
        router_forward(core).start()
        for copy in neighbour:
            copy.wait_recv()
            copy.wait_send()
        ids_out[...] = jnp.where(core == 0, ids[...], ids_near[...])
        ids_back[...] = jnp.where(core == 0, ids_near[...], ids[...])
        gain_out[...] = jnp.where(core == 0, gain_row[...], gain_near[...])
        round_router(core)
        for load in loads:
            load.wait()

    def router_here():
        router_forward(core).wait_send()
        router_forward(other).wait_recv()
        round_router(other)

    def down_here():
        for j in range(chips):
            copy = remote(wd_ref.at[:, pl.ds(0, LANES)], w_dn.at[other, j], wd_send.at[j], wd_recv.at[j], sibling)
            copy.wait_send()
            copy.wait_recv()

    group_count = len(groups)

    def group_work(moment, source, g, fresh):
        start, stop = groups[g]
        ks = range(start, stop)
        blocks = [x_in[moment, source, k] for k in ks]
        block = jnp.concatenate(blocks, axis=1)
        weight = jnp.concatenate([w_gu[source, place_of(order[k], -1)] for k in ks], axis=0)
        product = dot(block, weight)
        router = rt_bf[source, :, start * LANES : stop * LANES]
        logits = dot_t(block, router)
        squares = None
        for k, piece in zip(ks, blocks):
            wide = piece.astype(F32)
            term = wide * wide * rt_in[source, k, 8:9, :]
            squares = term if squares is None else squares + term
        if fresh:
            acc[...] = product
            logit_acc[...] = logits
            sq_acc[...] = squares
        else:
            acc[...] += product
            logit_acc[...] += logits
            sq_acc[...] += squares

    def forward_copy(source, g, moment):
        block = x_in.at[moment, source, pl.ds(groups[g][0], groups[g][1] - groups[g][0])]
        return remote(block, block, f_send.at[g], f_recv.at[g], sibling)

    def own_group(g, moment, fresh=False):
        if g == 0:

            @pl.when(jnp.logical_not(stays(moment)))
            def _():
                dispatch_copy(0, moment).wait_recv()

        for k in range(max(1, groups[g][0]), groups[g][1]):
            dispatch_copy(k, moment).wait_recv()
        forward_copy(core, g, moment).start()

    def sibling_group(g, moment):
        forward_copy(other, g, moment).wait_recv()
        group_work(moment, other, g, False)

    pairs = [tuple(range(n, n + spread_out)) for n in range(0, chips, spread_out)]

    def tick(moment, carry):
        dispatch(moment)
        ahead = remote(
            x_all.at[moment], x_res.at[moment], z_send.at[0], z_recv.at[moment], device((0, 0), 1)
        )
        ahead.start()

        @pl.when(moment == 0)
        def _():
            first_tick()

        prepare_mask(moment)
        prepare_scatter(moment)

        own_group(0, moment, True)
        for g in range(1, group_count):
            own_group(g, moment)
        for g in range(group_count):
            group_work(moment, core, g, g == 0)
        pl.when(moment == 0)(router_here)
        for g in range(group_count):
            sibling_group(g, moment)

        row_scale = lax.rsqrt(jnp.sum(sq_acc[...], axis=1, keepdims=True) / width + 1e-6)
        gate_part = acc[:, 0:hidden] * row_scale
        up_part = acc[:, hidden : 2 * hidden] * row_scale
        act[core] = (gate_part / (1.0 + jnp.exp(-gate_part)) * up_part).astype(BF16)
        swap = remote(act.at[core], act.at[core], a_send.at[0], a_recv.at[0], sibling)
        swap.start()

        chosen = chosen_mask[...] > 0.5
        logits = logit_acc[...] * row_scale
        lanes = lax.broadcasted_iota(jnp.int32, (slots, 16), 1)
        top = jnp.max(jnp.where(chosen, logits, -1e30), axis=1, keepdims=True)
        raised = jnp.where(chosen, jnp.exp(jnp.where(chosen, logits - top, 0.0)), 0.0)
        gate = jnp.sum(jnp.where(lanes == expert, raised, 0.0), axis=1, keepdims=True) / jnp.maximum(
            jnp.sum(raised, axis=1, keepdims=True), 1e-30
        )

        def down_weight(source, pair):
            return jnp.concatenate([w_dn[source, place_of(sends[n])] for n in pair], axis=1)

        own_act = act[core]
        for i, pair in enumerate(pairs):
            dn_acc[i] = dot(own_act, down_weight(core, pair))
        @pl.when(moment == 0)
        def _():
            down_here()

        remote(act.at[other], act.at[other], a_send.at[0], a_recv.at[0], sibling).wait_recv()
        sib_act = act[other]
        landing = half * experts + expert

        def part_copy(n):
            return remote(
                part_out.at[n, pl.ds(0, sent)], part_in.at[moment, landing, pl.ds(0, sent)], c_send.at[n],
                c_own.at[moment] if n == chips - 1 else c_recv.at[moment], device(sends[n], 1 - core),
            )

        for i, pair in enumerate(pairs):
            piece = ((dn_acc[i] + dot(sib_act, down_weight(other, pair))) * gate).astype(BF16)
            for at, n in enumerate(pair):
                value = piece[:, at * LANES : (at + 1) * LANES]
                part_out[n] = value
                if n < chips - 1:
                    part_copy(n).start()
                else:

                    @pl.when(core == 0)
                    def _(n=n):
                        part_copy(n).start()

                    @pl.when(core == 1)
                    def _(value=value):
                        part_in[moment, landing, 0:sent, :] = value[0:sent, :]

        prepare_pick(ids_out, micro_of(section + core - moment - 1))

        swap.wait_send()
        for g in range(group_count):
            forward_copy(core, g, moment).wait_send()
        for k in range(1, chips):
            dispatch_copy(k, moment).wait_send()

        @pl.when(jnp.logical_not(stays(moment)))
        def _():
            dispatch_copy(0, moment).wait_send()

        for n in range(chips - 1):
            part_copy(n).wait_send()

        @pl.when(core == 0)
        def _():
            part_copy(chips - 1).wait_send()
            part_copy(chips - 1).wait_recv()

        ahead.wait_send()
        ahead.wait_recv()
        everything = part_in.at[moment, pl.ds(0, chips - 1), pl.ds(0, sent)]
        remote(everything, everything, c_send.at[0], c_recv.at[moment], device((0, 0), 1)).wait_recv()
        table = scat[...]
        count = experts * slots
        parts = part_in[moment].reshape(chips * slots, LANES)
        moe = dot(table, parts[0:count]) + dot(table, parts[count : 2 * count])
        kept = jnp.where(core * (1 - begun(moment)) == 1, x_all[0].astype(F32), x_res[moment].astype(F32))
        x_all[moment + 1] = (kept + moe).astype(BF16)
        return carry

    lax.fori_loop(0, sections, tick, 0)

    last = remote(x_all.at[sections], x_last, l_send.at[0], l_recv.at[0], device((0, 0), 1))
    last.start()
    lanes = lax.broadcasted_iota(jnp.int32, (rows, LANES), 1).astype(F32)

    def members(group_row):
        column = dot_t(eye[...], jnp.broadcast_to(group_row.astype(F32), (16, rows)).astype(BF16))[:, 0:1]
        return jnp.where(column == lanes, 1.0, 0.0)

    aim = jnp.where(core == 0, tgt[...].astype(F32), tgt_near[...].astype(F32))
    error = x_all[sections].astype(F32) - aim
    row_loss = jnp.sum(error * error, axis=1, keepdims=True) / width
    belongs = members(jnp.where(core == 0, gid[...], gid_near[...]))
    totals = jnp.sum(belongs * row_loss, axis=0, keepdims=True)
    counts = jnp.sum(belongs, axis=0, keepdims=True)
    red_rows = lax.broadcasted_iota(jnp.int32, (8, LANES), 0)
    local = jnp.where(red_rows == 0, totals, counts)
    red_mine[0] = local
    red_in[mine] = local

    def plane_copy(k, place):
        return remote(red_mine.at[0], red_in.at[place], s_send.at[k], s_recv.at[k], device(order[k]))

    for k in range(1, chips):
        plane_copy(k, mine).start()
    own_members = members(gid[...])
    for k in range(1, chips):
        copy = plane_copy(k, place_of(order[k], -1))
        copy.wait_recv()
        copy.wait_send()
    plane = red_in[0]
    for j in range(1, chips):
        plane = plane + red_in[j]
    red_mine[1] = plane
    red_z[core, section] = plane
    steps = [(dz, swap) for dz in range(sections) for swap in range(2) if dz or swap]

    def depth_copy(n, lane_core, place):
        dz, swap = steps[n]
        return remote(
            red_mine.at[1], red_z.at[lane_core, place], sz_send.at[n], sz_recv.at[n], device((0, 0), dz, swap)
        )

    for n in range(len(steps)):
        depth_copy(n, core, section).start()
    for n, (dz, swap) in enumerate(steps):
        copy = depth_copy(n, other if swap else core, lax.rem(section + sections - dz, sections))
        copy.wait_recv()
        copy.wait_send()
    whole = red_z[0, 0]
    for n in range(1, 2 * sections):
        whole = whole + red_z[n // sections, n % sections]
    total = whole[0:1, :]
    count = whole[1:2, :] / (chips * 2)
    safe = jnp.maximum(count, 1.0)
    group_loss = total / safe
    lane_row = lax.broadcasted_iota(jnp.int32, (1, LANES), 1)
    raised = jnp.where(lane_row < GROUPS, jnp.exp(DRO_RATE * group_loss), 0.0)
    weight = raised / jnp.sum(raised, axis=1, keepdims=True) * (sections * rows) / safe
    row_weight = jnp.sum(own_members * weight, axis=1, keepdims=True)
    last.wait_send()
    last.wait_recv()
    final = jnp.where(core == 0, x_all[sections].astype(F32), x_last[...].astype(F32))
    difference = final - tgt[...].astype(F32)
    grad_ref[...] = (row_weight * difference).astype(BF16)
    loss_ref[...] = group_loss[:, 0:GROUPS]


def per_device(
    slots, sent, groups, spread_out, tokens, targets, group_ids, expert_ids, norm_gain, router, w_gate, w_up, w_down
):
    sections = lax.axis_size("section")
    experts = lax.axis_size("expert")
    chips = experts * 2
    rows = tokens.shape[1]
    width = w_gate.shape[2]
    hidden = w_gate.shape[3]
    choices = jnp.transpose(expert_ids[0, 0], (0, 2, 1))
    router_rows = jnp.transpose(router[0])
    if experts < 8:
        router_rows = jnp.zeros((8, LANES), BF16).at[:experts].set(router_rows)
    vmem = pl.BlockSpec(memory_space=pltpu.VMEM)
    anywhere = pl.BlockSpec(memory_space=pl.ANY)
    dma = pltpu.SemaphoreType.DMA
    scratch = [
        pltpu.VMEM((2, chips, LANES, 2 * hidden), BF16),
        pltpu.VMEM((2, chips, hidden, LANES), BF16),
        pltpu.VMEM((sections + 1, rows, LANES), BF16),
        pltpu.VMEM((sections, rows, LANES), BF16),
        pltpu.VMEM((experts * slots, LANES), BF16),
        pltpu.VMEM((sections, 2, chips, slots, LANES), BF16),
        pltpu.VMEM((slots, 2 * hidden), F32),
        pltpu.VMEM((slots, LANES), F32),
        pltpu.VMEM((slots, 16), F32),
        pltpu.VMEM((2, slots, hidden), BF16),
        pltpu.VMEM((chips // spread_out, slots, spread_out * LANES), F32),
        pltpu.VMEM((chips, slots, LANES), BF16),
        pltpu.VMEM((sections, chips, slots, LANES), BF16),
        pltpu.VMEM((rows, LANES), BF16),
        pltpu.VMEM((1, rows), jnp.int32),
        pltpu.VMEM((sections, 2, rows), jnp.int32),
        pltpu.VMEM((1, LANES), F32),
        pltpu.VMEM((8, LANES), BF16),
        pltpu.VMEM((rows, LANES), BF16),
        pltpu.VMEM((1, rows), jnp.int32),
        pltpu.VMEM((sections, 2, rows), jnp.int32),
        pltpu.VMEM((1, LANES), F32),
        pltpu.VMEM((sections, 2, rows), jnp.int32),
        pltpu.VMEM((sections, 2, rows), jnp.int32),
        pltpu.VMEM((1, LANES), F32),
        pltpu.VMEM((rows, LANES), BF16),
        pltpu.VMEM((experts * slots, rows), BF16),
        pltpu.VMEM((rows, experts * slots), BF16),
        pltpu.VMEM((slots, 16), F32),
        pltpu.VMEM((rows, rows), BF16),
        pltpu.VMEM((rows, rows), BF16),
        pltpu.VMEM((16, LANES), F32),
        pltpu.VMEM((2, chips, 16, LANES), F32),
        pltpu.VMEM((2, 16, chips * LANES), BF16),
        pltpu.VMEM((2, 8, LANES), F32),
        pltpu.VMEM((chips, 8, LANES), F32),
        pltpu.VMEM((2, sections, 8, LANES), F32),
        dma((6,)),
        dma((4,)),
        dma((chips,)),
        dma((chips,)),
        dma((chips,)),
        dma((chips,)),
        dma((sections, chips)),
        dma((len(groups),)),
        dma((len(groups),)),
        dma((1,)),
        dma((1,)),
        dma((chips,)),
        dma((sections,)),
        dma((sections,)),
        dma((1,)),
        dma((sections,)),
        dma((chips,)),
        dma((chips,)),
        dma((1,)),
        dma((1,)),
        dma((4,)),
        dma((4,)),
        dma((chips,)),
        dma((chips,)),
        dma((2 * sections - 1,)),
        dma((2 * sections - 1,)),
        dma((1,)),
        dma((1,)),
    ]
    grad, loss = pl.pallas_call(
        functools.partial(kernel, sections, experts, slots, sent, groups, spread_out, float(width)),
        out_shape=(
            jax.ShapeDtypeStruct((rows, LANES), BF16),
            jax.ShapeDtypeStruct((1, GROUPS), F32),
        ),
        in_specs=[anywhere] * 9,
        out_specs=(vmem, vmem),
        scratch_shapes=scratch,
        compiler_params=pltpu.CompilerParams(
            collective_id=0, has_side_effects=True, vmem_limit_bytes=60 * 1024 * 1024
        ),
        name="moe_ring",
    )(
        tokens[0],
        targets[0],
        group_ids,
        choices,
        norm_gain,
        router_rows,
        w_gate.reshape(chips, 2, LANES, hidden),
        w_up.reshape(chips, 2, LANES, hidden),
        w_down.reshape(hidden, width),
    )
    return grad[None], loss[0]


def build(mesh, slots, sent, groups, spread_out):
    placed = (
        P("section", None, ("expert", "dp")),
        P("section", None, ("expert", "dp")),
        P("section", None),
        P(None, "section", None, None, None),
        P("section", ("expert", "dp")),
        P("section", ("expert", "dp"), None),
        P("section", "expert", None, "dp"),
        P("section", "expert", None, "dp"),
        P("section", "expert", "dp", None),
    )
    return jax.shard_map(
        functools.partial(per_device, slots, sent, groups, spread_out),
        mesh=mesh,
        in_specs=placed,
        out_specs=(P("section", None, ("expert", "dp")), P()),
        check_vma=False,
    )


def solution(mesh):
    return build(mesh, 80, 72, ((0, 8), (8, 16)), 4)
```
